32 devices in a mesh: tile: 16 (over z, y, x), chan: 2 (over core).
Axes of the slice: x: 2, y: 2, z: 4, core: 2. Of those that a mesh axis runs over, the one named last changes fastest.
Arguments:
- tile_features: bfloat16 [128, 128, 1024], P('tile', 'chan'), may hold values from -6 to 6
- conv_weight: bfloat16 [128, 128, 3, 3], P('chan'), may hold values from -0.1875 to 0.1875
- merge_weight: bfloat16 [128, 4, 256], replicated, may hold values from -0.25 to 0.25
- tissue: int32 [128], P('tile'), may hold values 0 or 1
- group_tiles: int32 [32, 4], P('tile'), may hold values from 0 to 127, as said below
- neighbours: int32 [32, 8], P('tile'), may hold values from -1 to 31, as said below
- merged_grad: bfloat16 [32, 256, 1024], P('tile', 'chan'), may hold values from -0.032958984 to 0.032958984
Outputs:
- merged: bfloat16 [32, 256, 1024], P('tile', 'chan')
- grad_conv: float32 [128, 128, 3, 3], replicated
- grad_merge: float32 [128, 4, 256], replicated
The draws below stay inside these ranges and needn't reach their ends.
Inputs may be any that keep to these rules, and one draw needn't show every extreme that they name: `group_tiles`: row g lists the tiles of group g at top-left, top-right, bottom-left and bottom-right; every tile stands in exactly one row, and all four are held by the device that holds group g (tile t on index t // 8 of tile, group g on index g // 2). `neighbours`: entry e of row g names the group beside group g in direction e (0 up, 1 down, 2 left, 3 right, 4 up-left, 5 up-right, 6 down-left, 7 down-right) on the same slide, or -1 where there is none. The relation is mutual: entry e of g names h exactly when entry o(e) of h names g, o swapping 0 with 1, 2 with 3, 4 with 7, 5 with 6. With p = g // 2 and r = g % 2, a named group is h = q * 2 + r + u, where u = -1, 1, 0, 0, -1, -1, 1, 1 and v = 0, 0, -1, 1, -1, 1, -1, 1 for e = 0 .. 7 and q = (p + v + 4 * u) modulo the size of tile. The entries of one device's groups name groups of any single other device at most 2 times, and some device reaches that count.
All inputs are finite; a program needn't handle non-finite values. No bound on the sum of `tissue` on one device may be relied on, other than what follows from the above.
Results may differ from the reference program's by a relative error of at most 0.0049.
Values may be sent and summed in bfloat16 or wider, within the bound.
A program may use at most 64 MiB of HBM per device.

```python
import jax
import jax.numpy as jnp
from jax import lax

C = 128
M = 256
PIX = 32
GROUPS_DEV = 2
GROUPS = 32
TILES = 128


def draw_group_tiles(key, part):
    devices = GROUPS // GROUPS_DEV
    per_device = 4 * GROUPS_DEV
    device_keys = jax.random.split(jax.random.fold_in(key, 7), devices)
    orders = jax.vmap(lambda one_key: jax.random.permutation(one_key, per_device))(device_keys)
    offsets = jnp.arange(devices, dtype=jnp.int32)[:, None] * per_device
    return (orders.astype(jnp.int32) + offsets).reshape(GROUPS, 4)


def draw_neighbours(key, part):
    devices = GROUPS // GROUPS_DEV
    cut_key = jax.random.fold_in(key, 11)
    columns = jnp.arange(devices, dtype=jnp.int32)
    cuts = jax.random.randint(cut_key, (devices,), 0, 2).astype(jnp.int32) * (columns % 4 == 3).astype(jnp.int32)
    slide = jnp.concatenate([jnp.zeros((1,), jnp.int32), jnp.cumsum(cuts)[:-1].astype(jnp.int32)])
    group_ids = jnp.arange(GROUPS, dtype=jnp.int32)
    row_index = group_ids % GROUPS_DEV
    label = group_ids // GROUPS_DEV
    column = (label - 4 * row_index) % devices
    row_step = jnp.array([-1, 1, 0, 0, -1, -1, 1, 1], dtype=jnp.int32)
    column_step = jnp.array([0, 0, -1, 1, -1, 1, -1, 1], dtype=jnp.int32)
    other_row = row_index[:, None] + row_step[None, :]
    other_column = column[:, None] + column_step[None, :]
    inside = (other_row >= 0) & (other_row < GROUPS_DEV) & (other_column >= 0) & (other_column < devices)
    clipped = jnp.clip(other_column, 0, devices - 1)
    inside = inside & (slide[clipped] == slide[column][:, None])
    other_label = (clipped + 4 * other_row) % devices
    other_id = other_label * GROUPS_DEV + other_row
    return jnp.where(inside, other_id, -1).astype(jnp.int32)


def plant(result, key, low, top_value):
    place = [jax.random.randint(jax.random.fold_in(key, axis), (), 0, length) for axis, length in enumerate(result.shape)]
    main_axis = result.shape.index(max(result.shape))
    beside = place[:main_axis] + [(place[main_axis] + 1) % result.shape[main_axis]] + place[main_axis + 1:]
    return result.at[tuple(place)].set(low).at[tuple(beside)].set(top_value)


def shard_levels(own_key, dims, pieces, least, high):
    factor_of = 1.0
    for axis_at, shards_of in pieces:
        draws = jax.random.uniform(jax.random.fold_in(jax.random.fold_in(own_key, 6), axis_at), (shards_of,), jnp.float32, least / len(pieces), high / len(pieces))
        factor_of = factor_of * jnp.repeat(jnp.exp(draws), dims[axis_at] // shards_of).reshape((-1,) + (1,) * (len(dims) - 1 - axis_at))
    return factor_of


def normal_values(key, shape, spread, limit, shards=(), kind=jnp.bfloat16):
    level = shard_levels(key, shape, shards, -0.22, 0.18) if shards else 1.0
    entries = jax.random.normal(key, shape, jnp.float32) * spread * level
    return jnp.minimum(jnp.maximum(entries, -limit), limit).astype(kind)


def setup_inputs(seed: int = 0) -> dict:
    key_list = jax.random.split(jax.random.key(seed), 8)
    return {
        "tile_features": normal_values(key_list[0], (TILES, C, PIX * PIX), 1.0, 6.0, ((0, 16), (1, 2))),
        "conv_weight": normal_values(key_list[1], (C, C, 3, 3), (9 * C) ** -0.5, 0.1875, ((0, 2),)),
        "merge_weight": normal_values(key_list[2], (C, 4, M), (4 * C) ** -0.5, 0.25),
        "tissue": plant((jax.random.randint(key_list[3], (TILES,), 0, 4) < 3).astype(jnp.int32), jax.random.fold_in(key_list[3], 1), 0, 1),
        "group_tiles": draw_group_tiles(jax.random.fold_in(key_list[7], 71), 0),
        "neighbours": draw_neighbours(jax.random.fold_in(key_list[7], 71), 0),
        "merged_grad": normal_values(key_list[6], (GROUPS, M, PIX * PIX), (1.0 / (GROUPS * PIX * PIX) ** 0.5), 0.032958984, ((0, 16), (1, 2))),
    }


OPPOSITE = (1, 0, 3, 2, 7, 6, 5, 4)


def boundary(picture):
    top_row = picture[:, :, 0, :]
    bottom_row = picture[:, :, -1, :]
    left_column = picture[:, :, :, 0]
    right_column = picture[:, :, :, -1]
    return jnp.stack([top_row, bottom_row, left_column, right_column, top_row, top_row, bottom_row, bottom_row], axis=1)


def assemble(tile_rows, local_ids, width):
    number = local_ids.shape[0]
    channels = tile_rows.shape[1]
    picked = jnp.take(tile_rows, local_ids.reshape(-1), axis=0)
    picked = picked.reshape(number, 2, 2, channels, width, width)
    return picked.transpose(0, 3, 1, 4, 2, 5).reshape(number, channels, 2 * width, 2 * width)


def framed(picture, rim_cells):
    extent = picture.shape[2]
    upper = jnp.concatenate([rim_cells[:, 4, :, extent - 1:], rim_cells[:, 0], rim_cells[:, 5, :, :1]], axis=2)
    lower = jnp.concatenate([rim_cells[:, 6, :, extent - 1:], rim_cells[:, 1], rim_cells[:, 7, :, :1]], axis=2)
    middle = jnp.concatenate([rim_cells[:, 2][..., None], picture, rim_cells[:, 3][..., None]], axis=3)
    return jnp.concatenate([upper[:, :, None, :], middle, lower[:, :, None, :]], axis=2)


def tissue_map(tissue_rows, width):
    number = tissue_rows.shape[0]
    layout = tissue_rows.reshape(number, 2, 1, 2, 1)
    return jnp.broadcast_to(layout, (number, 2, width, 2, width)).reshape(number, 2 * width, 2 * width)


def to_blocks(hidden, width):
    number, channels = hidden.shape[0], hidden.shape[1]
    shaped = hidden.reshape(number, channels, width, 2, width, 2)
    return shaped.transpose(0, 3, 5, 1, 2, 4).reshape(number, 4, channels, width * width)


def from_blocks(blocks, width):
    number, channels = blocks.shape[0], blocks.shape[2]
    shaped = blocks.reshape(number, 2, 2, channels, width, width)
    return shaped.transpose(0, 3, 4, 1, 5, 2).reshape(number, channels, 2 * width, 2 * width)


def reference(tile_features, conv_weight, merge_weight, tissue, group_tiles, neighbours, merged_grad):
    block_count = GROUPS // GROUPS_DEV
    extent = 2 * PIX
    tile_ids = group_tiles.reshape(block_count, GROUPS_DEV, 4)
    edge_all = lax.map(lambda one_ids: boundary(assemble(tile_features, one_ids, PIX)), tile_ids)
    edge_all = edge_all.reshape(GROUPS, 8, C, extent)
    opposite = jnp.array(OPPOSITE, dtype=jnp.int32)
    safe_ids = jnp.maximum(neighbours, 0)
    rim_all = edge_all[safe_ids, opposite[None, :]]
    rim_all = jnp.where((neighbours >= 0)[:, :, None, None], rim_all, jnp.zeros((), rim_all.dtype))
    tissue_rows = tissue[group_tiles].astype(jnp.float32)
    weight_conv = conv_weight.astype(jnp.float32)
    weight_merge = merge_weight.astype(jnp.float32)
    highest = lax.Precision.HIGHEST

    def one_block(totals, inputs):
        block_ids, rim_cells, tissue_block, grad_block = inputs
        padded = framed(assemble(tile_features, block_ids, PIX), rim_cells).astype(jnp.float32)
        conv_out = lax.conv_general_dilated(padded, weight_conv, (1, 1), "VALID", dimension_numbers=("NCHW", "OIHW", "NCHW"), precision=highest)
        hidden = (jnp.maximum(conv_out, 0.0) * tissue_map(tissue_block, PIX)[:, None]).astype(jnp.bfloat16)
        hidden_blocks = to_blocks(hidden, PIX).astype(jnp.float32)
        merged = jnp.einsum("ckm,gkcq->gmq", weight_merge, hidden_blocks, precision=highest).astype(jnp.bfloat16)
        upstream = grad_block.astype(jnp.float32)
        grad_hidden = from_blocks(jnp.einsum("ckm,gmq->gkcq", weight_merge, upstream, precision=highest), PIX)
        grad_pre = jnp.where(hidden > 0, grad_hidden, 0.0).astype(jnp.bfloat16)
        merge_term = jnp.einsum("gmq,gkcq->ckm", upstream, hidden_blocks, precision=highest)
        conv_term = lax.conv_general_dilated(padded, grad_pre.astype(jnp.float32), (1, 1), "VALID", dimension_numbers=("CNHW", "IOHW", "NCHW"), precision=highest)
        return (totals[0] + conv_term.transpose(1, 0, 2, 3), totals[1] + merge_term), merged

    inputs = (tile_ids, rim_all.reshape(block_count, GROUPS_DEV, 8, C, extent), tissue_rows.reshape(block_count, GROUPS_DEV, 4), merged_grad.reshape(block_count, GROUPS_DEV, M, PIX * PIX))
    start = (jnp.zeros((C, C, 3, 3), jnp.float32), jnp.zeros((C, 4, M), jnp.float32))
    totals, merged_all = lax.scan(one_block, start, inputs)
    return merged_all.reshape(GROUPS, M, PIX * PIX), totals[0], totals[1]
```

```python
import jax
import jax.numpy as jnp
from jax import lax
from jax.experimental import pallas as pl
from jax.experimental.pallas import tpu as pltpu
from jax.sharding import PartitionSpec as P

PIX = 32


OPPOSITE = (1, 0, 3, 2, 7, 6, 5, 4)
ROW_STEPS = (-1, 1, 0, 0, -1, -1, 1, 1)
COLUMN_STEPS = (0, 0, -1, 1, -1, 1, -1, 1)


def passed_along(block, axis, distance):
    devices = range(lax.axis_size(axis))
    route = [((i - distance) % len(devices), i) for i in devices]
    return lax.ppermute(block, axis, route)


def boundary(picture):
    top_row = picture[:, :, 0, :]
    bottom_row = picture[:, :, -1, :]
    left_column = picture[:, :, :, 0]
    right_column = picture[:, :, :, -1]
    return jnp.stack(
        [top_row, bottom_row, left_column, right_column, top_row, top_row, bottom_row, bottom_row],
        axis=1,
    )


def assemble(tile_rows, local_ids, width):
    number = local_ids.shape[0]
    channels = tile_rows.shape[1]
    picked = jnp.take(tile_rows, local_ids.reshape(-1), axis=0)
    picked = picked.reshape(number, 2, 2, channels, width, width)
    return picked.transpose(0, 3, 1, 4, 2, 5).reshape(number, channels, 2 * width, 2 * width)


def framed(picture, rim_cells):
    extent = picture.shape[2]
    upper = jnp.concatenate(
        [rim_cells[:, 4, :, extent - 1 :], rim_cells[:, 0], rim_cells[:, 5, :, :1]], axis=2
    )
    lower = jnp.concatenate(
        [rim_cells[:, 6, :, extent - 1 :], rim_cells[:, 1], rim_cells[:, 7, :, :1]], axis=2
    )
    middle = jnp.concatenate(
        [rim_cells[:, 2][..., None], picture, rim_cells[:, 3][..., None]], axis=3
    )
    return jnp.concatenate([upper[:, :, None, :], middle, lower[:, :, None, :]], axis=2)


def tissue_map(tissue_rows, width):
    number = tissue_rows.shape[0]
    layout = tissue_rows.reshape(number, 2, 1, 2, 1)
    return jnp.broadcast_to(layout, (number, 2, width, 2, width)).reshape(
        number, 2 * width, 2 * width
    )


def to_blocks(hidden, width):
    number, channels = (hidden.shape[0], hidden.shape[1])
    shaped = hidden.reshape(number, channels, width, 2, width, 2)
    return shaped.transpose(0, 3, 5, 1, 2, 4).reshape(number, 4, channels, width * width)


def from_blocks(blocks, width):
    number, channels = (blocks.shape[0], blocks.shape[2])
    shaped = blocks.reshape(number, 2, 2, channels, width, width)
    return shaped.transpose(0, 3, 4, 1, 5, 2).reshape(number, channels, 2 * width, 2 * width)


MESH = pl.DeviceIdType.MESH
LANES = 128


def total_kernel(n, nc, part_ref, out_ref, recv, send_a, recv_a, send_b, recv_b, send_c, recv_c):
    me = lax.axis_index("tile")
    core = lax.axis_index("chan")
    barrier = pltpu.get_barrier_semaphore()
    for d in range(1, n):
        pl.semaphore_signal(
            barrier, inc=1, device_id=(lax.rem(me + d, n), core), device_id_type=MESH
        )
    for d in range(1, nc):
        pl.semaphore_signal(
            barrier, inc=1, device_id=(me, lax.rem(core + d, nc)), device_id_type=MESH
        )
    pl.semaphore_wait(barrier, n - 1 + nc - 1)

    scatter = []
    for d in range(1, n):
        peer = lax.rem(me + d, n)
        copy = pltpu.make_async_remote_copy(
            src_ref=part_ref.at[peer],
            dst_ref=recv.at[d],
            send_sem=send_a.at[d],
            recv_sem=recv_a.at[d],
            device_id=(peer, core),
            device_id_type=MESH,
        )
        copy.start()
        scatter.append(copy)
    total = part_ref[me].astype(jnp.float32)
    for d in range(1, n):
        scatter[d - 1].wait_recv()
        total += recv[d].astype(jnp.float32)
    out_ref[core, me] = total.astype(out_ref.dtype)

    spread = []
    for d in range(1, n):
        copy = pltpu.make_async_remote_copy(
            src_ref=out_ref.at[core, me],
            dst_ref=out_ref.at[core, me],
            send_sem=send_b.at[d],
            recv_sem=recv_b.at[d],
            device_id=(lax.rem(me + d, n), core),
            device_id_type=MESH,
        )
        copy.start()
        spread.append(copy)
    for copy in spread:
        copy.wait_recv()
    crossing = []
    for d in range(1, nc):
        copy = pltpu.make_async_remote_copy(
            src_ref=out_ref.at[core],
            dst_ref=out_ref.at[core],
            send_sem=send_c.at[d],
            recv_sem=recv_c.at[d],
            device_id=(me, lax.rem(core + d, nc)),
            device_id_type=MESH,
        )
        copy.start()
        crossing.append(copy)
    for copy in scatter + spread:
        copy.wait_send()
    for copy in crossing:
        copy.wait()


def totals(parts, n, nc):
    rows = parts.shape[1]
    return pl.pallas_call(
        lambda *refs: total_kernel(n, nc, *refs),
        name="weight_totals",
        out_shape=jax.ShapeDtypeStruct((nc, n, rows, LANES), parts.dtype),
        in_specs=[pl.BlockSpec(memory_space=pltpu.VMEM)],
        out_specs=pl.BlockSpec(memory_space=pltpu.VMEM),
        scratch_shapes=[pltpu.VMEM((n, rows, LANES), parts.dtype)]
        + [pltpu.SemaphoreType.DMA((n,))] * 4
        + [pltpu.SemaphoreType.DMA((nc,))] * 2,
        compiler_params=pltpu.CompilerParams(collective_id=0, has_side_effects=True),
    )(parts)


def shards(tile_features, conv_weight, merge_weight, tissue, group_tiles, neighbours, merged_grad):
    chan_index = lax.axis_index("chan")
    local_groups = neighbours.shape[0]
    local_tiles = tile_features.shape[0]
    own_chan = tile_features.shape[1]
    own_merged = merged_grad.shape[1]
    extent = 2 * PIX
    local_ids = group_tiles % local_tiles
    own_picture = assemble(tile_features, local_ids, PIX)
    own_edges = boundary(own_picture)
    sides = []
    for direction in range(8):
        row_step = ROW_STEPS[direction]
        device_step = COLUMN_STEPS[direction] + 4 * row_step
        sending = own_edges[:, OPPOSITE[direction]]
        arrived = passed_along(sending, "tile", -device_step)
        blank = jnp.zeros((1, own_chan, extent), jnp.bfloat16)
        if row_step == 1:
            aligned = jnp.concatenate([arrived[1:], blank], axis=0)
        elif row_step == -1:
            aligned = jnp.concatenate([blank, arrived[:-1]], axis=0)
        else:
            aligned = arrived
        present_rows = (neighbours[:, direction] >= 0)[:, None, None]
        sides.append(jnp.where(present_rows, aligned, jnp.zeros((), jnp.bfloat16)))
    rim_flat = jnp.stack(sides, axis=2).reshape(local_groups, own_chan, 8 * extent)
    all_tiles, all_rims = (
        lax.all_gather(tile_features, "chan", axis=1, tiled=True),
        lax.all_gather(rim_flat, "chan", axis=1, tiled=True),
    )
    channels_all = all_tiles.shape[1]
    rim_cells = all_rims.reshape(local_groups, channels_all, 8, extent).transpose(0, 2, 1, 3)
    padded = framed(assemble(all_tiles, local_ids, PIX), rim_cells)
    conv_out = lax.conv_general_dilated(
        padded,
        conv_weight,
        (1, 1),
        "VALID",
        dimension_numbers=("NCHW", "OIHW", "NCHW"),
        preferred_element_type=jnp.float32,
    )
    tissue_rows = (
        jnp.take(tissue, local_ids.reshape(-1)).reshape(local_groups, 4).astype(jnp.float32)
    )
    hidden = (jnp.maximum(conv_out, 0.0) * tissue_map(tissue_rows, PIX)[:, None]).astype(
        jnp.bfloat16
    )
    hidden_blocks = to_blocks(hidden, PIX)
    merge_rows = lax.dynamic_slice_in_dim(merge_weight, chan_index * own_chan, own_chan, 0)
    every_block = lax.all_gather(hidden_blocks, "chan", axis=2, tiled=True)
    merge_columns = lax.dynamic_slice_in_dim(merge_weight, chan_index * own_merged, own_merged, 2)
    merged = jnp.einsum(
        "ckm,gkcq->gmq", merge_columns, every_block, preferred_element_type=jnp.float32
    ).astype(jnp.bfloat16)
    upstream = lax.all_gather(merged_grad, "chan", axis=1, tiled=True)
    grad_hidden = from_blocks(
        jnp.einsum("ckm,gmq->gkcq", merge_rows, upstream, preferred_element_type=jnp.float32), PIX
    )
    grad_pre = jnp.where(hidden > 0, grad_hidden, 0.0).astype(jnp.bfloat16)
    merge_term = jnp.einsum(
        "gmq,gkcq->ckm", upstream, hidden_blocks, preferred_element_type=jnp.float32
    )
    conv_term = lax.conv_general_dilated(
        padded,
        grad_pre,
        (1, 1),
        "VALID",
        dimension_numbers=("CNHW", "IOHW", "NCHW"),
        preferred_element_type=jnp.float32,
    )
    conv_term = conv_term.transpose(1, 0, 2, 3)
    n = lax.axis_size("tile")
    nc = lax.axis_size("chan")
    conv_rows = conv_term.transpose(2, 3, 0, 1).reshape(-1, LANES)
    merge_rows_part = merge_term.reshape(-1, LANES)
    stacked = jnp.concatenate([conv_rows, merge_rows_part], axis=0).astype(jnp.bfloat16)
    used = stacked.shape[0]
    rows = -(-used // (16 * n)) * 16
    parts = jnp.pad(stacked, ((0, rows * n - used), (0, 0))).reshape(n, rows, LANES)
    summed = totals(parts, n, nc).reshape(nc, n * rows, LANES)
    conv_count = conv_rows.shape[0]
    grad_conv = (
        summed[:, :conv_count]
        .reshape(nc, 3, 3, own_chan, channels_all)
        .transpose(0, 3, 4, 1, 2)
        .reshape(channels_all, channels_all, 3, 3)
        .astype(jnp.float32)
    )
    grad_merge = (
        summed[:, conv_count:used].reshape(merge_weight.shape).astype(jnp.float32)
    )
    return (merged, grad_conv, grad_merge)


def solution(mesh):
    placed = (
        P("tile", "chan", None),
        P("chan", None, None, None),
        P(),
        P("tile"),
        P("tile", None),
        P("tile", None),
        P("tile", "chan", None),
    )
    return jax.shard_map(
        shards,
        mesh=mesh,
        in_specs=placed,
        out_specs=(P("tile", "chan", None), P(), P()),
        check_vma=False,
    )
```

```python
import jax
import ml_dtypes
import numpy as np
import jax.numpy as jnp
from jax import lax
from jax.experimental import pallas as pl
from jax.experimental.pallas import tpu as pltpu
from jax.sharding import PartitionSpec as P

PIX = 32


OPPOSITE = (1, 0, 3, 2, 7, 6, 5, 4)
ROW_STEPS = (-1, 1, 0, 0, -1, -1, 1, 1)
COLUMN_STEPS = (0, 0, -1, 1, -1, 1, -1, 1)


def passed_along(block, axis, distance):
    devices = range(lax.axis_size(axis))
    route = [((i - distance) % len(devices), i) for i in devices]
    return lax.ppermute(block, axis, route)


def boundary(picture):
    top_row = picture[:, :, 0, :]
    bottom_row = picture[:, :, -1, :]
    left_column = picture[:, :, :, 0]
    right_column = picture[:, :, :, -1]
    return jnp.stack(
        [top_row, bottom_row, left_column, right_column, top_row, top_row, bottom_row, bottom_row],
        axis=1,
    )


def assemble(tile_rows, local_ids, width):
    number = local_ids.shape[0]
    channels = tile_rows.shape[1]
    picked = jnp.take(tile_rows, local_ids.reshape(-1), axis=0)
    picked = picked.reshape(number, 2, 2, channels, width, width)
    return picked.transpose(0, 3, 1, 4, 2, 5).reshape(number, channels, 2 * width, 2 * width)


def framed(picture, rim_cells):
    extent = picture.shape[2]
    upper = jnp.concatenate(
        [rim_cells[:, 4, :, extent - 1 :], rim_cells[:, 0], rim_cells[:, 5, :, :1]], axis=2
    )
    lower = jnp.concatenate(
        [rim_cells[:, 6, :, extent - 1 :], rim_cells[:, 1], rim_cells[:, 7, :, :1]], axis=2
    )
    middle = jnp.concatenate(
        [rim_cells[:, 2][..., None], picture, rim_cells[:, 3][..., None]], axis=3
    )
    return jnp.concatenate([upper[:, :, None, :], middle, lower[:, :, None, :]], axis=2)


def tissue_map(tissue_rows, width):
    number = tissue_rows.shape[0]
    layout = tissue_rows.reshape(number, 2, 1, 2, 1)
    return jnp.broadcast_to(layout, (number, 2, width, 2, width)).reshape(
        number, 2 * width, 2 * width
    )


def to_blocks(hidden, width):
    number, channels = (hidden.shape[0], hidden.shape[1])
    shaped = hidden.reshape(number, channels, width, 2, width, 2)
    return shaped.transpose(0, 3, 5, 1, 2, 4).reshape(number, 4, channels, width * width)


def from_blocks(blocks, width):
    number, channels = (blocks.shape[0], blocks.shape[2])
    shaped = blocks.reshape(number, 2, 2, channels, width, width)
    return shaped.transpose(0, 3, 4, 1, 5, 2).reshape(number, channels, 2 * width, 2 * width)


MESH = pl.DeviceIdType.MESH
LANES = 128


def total_kernel(n, nc, part_ref, out_ref, recv, send_a, recv_a, send_b, recv_b, send_c, recv_c):
    me = lax.axis_index("tile")
    core = lax.axis_index("chan")
    barrier = pltpu.get_barrier_semaphore()
    for d in range(1, n):
        pl.semaphore_signal(
            barrier, inc=1, device_id=(lax.rem(me + d, n), core), device_id_type=MESH
        )
    for d in range(1, nc):
        pl.semaphore_signal(
            barrier, inc=1, device_id=(me, lax.rem(core + d, nc)), device_id_type=MESH
        )
    pl.semaphore_wait(barrier, n - 1 + nc - 1)

    scatter = []
    for d in range(1, n):
        peer = lax.rem(me + d, n)
        copy = pltpu.make_async_remote_copy(
            src_ref=part_ref.at[peer],
            dst_ref=recv.at[d],
            send_sem=send_a.at[d],
            recv_sem=recv_a.at[d],
            device_id=(peer, core),
            device_id_type=MESH,
        )
        copy.start()
        scatter.append(copy)
    total = part_ref[me].astype(jnp.float32)
    for d in range(1, n):
        scatter[d - 1].wait_recv()
        total += recv[d].astype(jnp.float32)
    out_ref[core, me] = total.astype(out_ref.dtype)

    spread = []
    for d in range(1, n):
        copy = pltpu.make_async_remote_copy(
            src_ref=out_ref.at[core, me],
            dst_ref=out_ref.at[core, me],
            send_sem=send_b.at[d],
            recv_sem=recv_b.at[d],
            device_id=(lax.rem(me + d, n), core),
            device_id_type=MESH,
        )
        copy.start()
        spread.append(copy)
    for copy in spread:
        copy.wait_recv()
    crossing = []
    for d in range(1, nc):
        copy = pltpu.make_async_remote_copy(
            src_ref=out_ref.at[core],
            dst_ref=out_ref.at[core],
            send_sem=send_c.at[d],
            recv_sem=recv_c.at[d],
            device_id=(me, lax.rem(core + d, nc)),
            device_id_type=MESH,
        )
        copy.start()
        crossing.append(copy)
    for copy in scatter + spread:
        copy.wait_send()
    for copy in crossing:
        copy.wait()


def totals(parts, n, nc):
    rows = parts.shape[1]
    return pl.pallas_call(
        lambda *refs: total_kernel(n, nc, *refs),
        name="weight_totals",
        out_shape=jax.ShapeDtypeStruct((nc, n, rows, LANES), parts.dtype),
        in_specs=[pl.BlockSpec(memory_space=pltpu.VMEM)],
        out_specs=pl.BlockSpec(memory_space=pltpu.VMEM),
        scratch_shapes=[pltpu.VMEM((n, rows, LANES), parts.dtype)]
        + [pltpu.SemaphoreType.DMA((n,))] * 4
        + [pltpu.SemaphoreType.DMA((nc,))] * 2,
        compiler_params=pltpu.CompilerParams(collective_id=0, has_side_effects=True),
    )(parts)


def shards(tile_features, conv_weight, merge_weight, tissue, group_tiles, neighbours, merged_grad):
    chan_index = lax.axis_index("chan")
    local_groups = neighbours.shape[0]
    local_tiles = tile_features.shape[0]
    own_chan = tile_features.shape[1]
    own_merged = merged_grad.shape[1]
    extent = 2 * PIX
    local_ids = group_tiles % local_tiles
    own_picture = assemble(tile_features, local_ids, PIX)
    own_edges = boundary(own_picture)
    sides = []
    for direction in range(8):
        row_step = ROW_STEPS[direction]
        device_step = COLUMN_STEPS[direction] + 4 * row_step
        sending = own_edges[:, OPPOSITE[direction]]
        arrived = passed_along(sending, "tile", -device_step)
        blank = jnp.zeros((1, own_chan, extent), jnp.bfloat16)
        if row_step == 1:
            aligned = jnp.concatenate([arrived[1:], blank], axis=0)
        elif row_step == -1:
            aligned = jnp.concatenate([blank, arrived[:-1]], axis=0)
        else:
            aligned = arrived
        present_rows = (neighbours[:, direction] >= 0)[:, None, None]
        sides.append(jnp.where(present_rows, aligned, jnp.zeros((), jnp.bfloat16)))
    rim_flat = jnp.stack(sides, axis=2).reshape(local_groups, own_chan, 8 * extent)
    all_tiles, all_rims = (
        lax.all_gather(tile_features, "chan", axis=1, tiled=True),
        lax.all_gather(rim_flat, "chan", axis=1, tiled=True),
    )
    channels_all = all_tiles.shape[1]
    rim_cells = all_rims.reshape(local_groups, channels_all, 8, extent).transpose(0, 2, 1, 3)
    padded = framed(assemble(all_tiles, local_ids, PIX), rim_cells)
    conv_out = lax.conv_general_dilated(
        padded,
        conv_weight,
        (1, 1),
        "VALID",
        dimension_numbers=("NCHW", "OIHW", "NCHW"),
        preferred_element_type=jnp.float32,
    )
    tissue_rows = (
        jnp.take(tissue, local_ids.reshape(-1)).reshape(local_groups, 4).astype(jnp.float32)
    )
    hidden = (jnp.maximum(conv_out, 0.0) * tissue_map(tissue_rows, PIX)[:, None]).astype(
        jnp.bfloat16
    )
    hidden_blocks = to_blocks(hidden, PIX)
    merge_rows = lax.dynamic_slice_in_dim(merge_weight, chan_index * own_chan, own_chan, 0)
    every_block = lax.all_gather(hidden_blocks, "chan", axis=2, tiled=True)
    merge_columns = lax.dynamic_slice_in_dim(merge_weight, chan_index * own_merged, own_merged, 2)
    merged = jnp.einsum(
        "ckm,gkcq->gmq", merge_columns, every_block, preferred_element_type=jnp.float32
    ).astype(jnp.bfloat16)
    upstream = lax.all_gather(merged_grad, "chan", axis=1, tiled=True)
    grad_hidden = from_blocks(
        jnp.einsum("ckm,gmq->gkcq", merge_rows, upstream, preferred_element_type=jnp.float32), PIX
    )
    grad_pre = jnp.where(hidden > 0, grad_hidden, 0.0).astype(jnp.bfloat16)
    merge_term = jnp.einsum(
        "gmq,gkcq->ckm", upstream, hidden_blocks, preferred_element_type=jnp.float32
    )
    conv_term = lax.conv_general_dilated(
        padded,
        grad_pre,
        (1, 1),
        "VALID",
        dimension_numbers=("CNHW", "IOHW", "NCHW"),
        preferred_element_type=jnp.float32,
    )
    conv_term = conv_term.transpose(1, 0, 2, 3)
    n = lax.axis_size("tile")
    nc = lax.axis_size("chan")
    conv_rows = conv_term.transpose(2, 3, 0, 1).reshape(-1, LANES)
    merge_rows_part = merge_term.reshape(-1, LANES)
    stacked = jnp.concatenate([conv_rows, merge_rows_part], axis=0).astype(jnp.bfloat16)
    used = stacked.shape[0]
    rows = -(-used // (16 * n)) * 16
    parts = jnp.pad(stacked, ((0, rows * n - used), (0, 0))).reshape(n, rows, LANES)
    summed = totals(parts, n, nc).reshape(nc, n * rows, LANES)
    conv_count = conv_rows.shape[0]
    grad_conv = (
        summed[:, :conv_count]
        .reshape(nc, 3, 3, own_chan, channels_all)
        .transpose(0, 3, 4, 1, 2)
        .reshape(channels_all, channels_all, 3, 3)
        .astype(jnp.float32)
    )
    grad_merge = (
        summed[:, conv_count:used].reshape(merge_weight.shape).astype(jnp.float32)
    )
    return (merged, grad_conv, grad_merge)


def edge_picker():
    picks = np.zeros((PIX * PIX, 4 * PIX), np.float32)
    for i in range(PIX):
        picks[i, i] = 1
        picks[(PIX - 1) * PIX + i, PIX + i] = 1
        picks[i * PIX, 2 * PIX + i] = 1
        picks[i * PIX + PIX - 1, 3 * PIX + i] = 1
    return picks.astype(ml_dtypes.bfloat16)


def phase_picker():
    picks = np.zeros((2, 8, PIX, 2, 2, 4, PIX), np.float32)
    for side in range(2):
        for row in range(8):
            for x in range(PIX):
                picks[side, row, x, row % 2, x % 2, row // 2, 16 * side + x // 2] = 1
    return picks.reshape(512, 512).astype(ml_dtypes.bfloat16)


def column_picker():
    picks = np.zeros((2, 4 * PIX, 2, 16, PIX), np.float32)
    for r in range(2):
        for y in range(16):
            picks[0, 3 * PIX + 2 * y + r, r, y, 0] = 1
            picks[1, 2 * PIX + 2 * y + r, r, y, PIX - 1] = 1
    return picks.reshape(256, 1024).astype(ml_dtypes.bfloat16)


def row_picker():
    picks = np.zeros((2, 4, 4 * PIX, 4, 128), np.float32)
    for core in range(2):
        base = PIX * core
        for t in range(4):
            for x in range(PIX):
                at = 2 * x + t
                out = x if core == 1 else 96 + x
                if at == 0:
                    slot, lane = 2, base + PIX - 1
                elif at == 65:
                    slot, lane = 3, base
                else:
                    slot, lane = (at - 1) // PIX, base + (at - 1) % PIX
                picks[core, slot, lane, t, out] = 1
    return picks.reshape(2, 512, 512).astype(ml_dtypes.bfloat16)


def exchange_kernel(
    n, tiles, grad, weight, edges, full, grad_full, weight_full, side, cap,
    send_own, recv_own, send_side, recv_side, send_cap, recv_cap,
):
    p = lax.axis_index("tile")
    k = lax.axis_index("chan")
    other = 1 - k
    toward = 1 - 2 * k
    barrier = pltpu.get_barrier_semaphore()

    def at(step):
        return lax.rem(p + step + n, n)

    def greet(row, core):
        pl.semaphore_signal(barrier, inc=1, device_id=(row, core), device_id_type=MESH)

    greet(p, other)
    for core in range(2):
        for step in (-1, 1):
            greet(at(step), core)
        for step in (3, 4, 5):
            greet(at(toward * step), core)
    pl.semaphore_wait(barrier, 11)

    def send(src, dst, send_sem, recv_sem, row, core):
        copy = pltpu.make_async_remote_copy(
            src_ref=src,
            dst_ref=dst,
            send_sem=send_sem,
            recv_sem=recv_sem,
            device_id=(row, core),
            device_id_type=MESH,
        )
        copy.start()
        return copy

    half = pl.ds(pl.multiple_of(64 * k, 64), 64)
    wide = pl.ds(pl.multiple_of(128 * k, 128), 128)
    copies = []
    for g in range(2):
        for s, step in ((0, 1), (1, -1)):
            copies.append(
                send(
                    edges.at[g, 1 - s], side.at[s, :, half],
                    send_side.at[g, s], recv_side.at[s, k], at(step), g,
                )
            )
    for target, sign in ((1, 1), (0, -1)):
        g = 1 - target
        copies.append(
            send(
                edges.at[g, :, target], cap.at[0:2, half],
                send_cap.at[target, 0], recv_cap.at[0, k], at(4 * sign), target,
            )
        )
        for slot, step, column in ((2, 5 if sign > 0 else -3, 1), (3, 3 if sign > 0 else -5, 0)):
            copies.append(
                send(
                    edges.at[g, column, target], cap.at[slot, half],
                    send_cap.at[target, slot - 1], recv_cap.at[slot - 1, k], at(step), target,
                )
            )
    copies.append(send(tiles.at[other], full.at[:, half], send_own.at[0], recv_own.at[0], p, other))
    copies.append(send(grad.at[other], grad_full.at[wide], send_own.at[1], recv_own.at[1], p, other))
    copies.append(send(weight, weight_full.at[k], send_own.at[2], recv_own.at[2], p, other))
    full[:, half] = tiles[k]
    grad_full[wide] = grad[k]
    weight_full[k] = weight[...]
    for copy in copies:
        copy.wait_send()
    copies[-1].wait_recv()
    copies[-2].wait_recv()
    copies[-3].wait_recv()

    def arrived(dst, recv_sem):
        pltpu.make_async_remote_copy(
            src_ref=dst,
            dst_ref=dst,
            send_sem=send_own.at[0],
            recv_sem=recv_sem,
            device_id=(p, other),
            device_id_type=MESH,
        ).wait_recv()

    for core in range(2):
        part = pl.ds(64 * core, 64)
        for s in range(2):
            arrived(side.at[s, :, part], recv_side.at[s, core])
        arrived(cap.at[0:2, part], recv_cap.at[0, core])
        arrived(cap.at[2, part], recv_cap.at[1, core])
        arrived(cap.at[3, part], recv_cap.at[2, core])


def exchange(tiles, grad, weight, edges, n):
    bf = jnp.bfloat16
    vmem = pl.BlockSpec(memory_space=pltpu.VMEM)
    return pl.pallas_call(
        lambda *refs: exchange_kernel(n, *refs),
        name="exchange",
        out_shape=(
            jax.ShapeDtypeStruct((4, 128, 1024), bf),
            jax.ShapeDtypeStruct((256, 1024), bf),
            jax.ShapeDtypeStruct((2, 9, 64, 128), bf),
            jax.ShapeDtypeStruct((2, 2, 128, 128), bf),
            jax.ShapeDtypeStruct((4, 128, 128), bf),
        ),
        in_specs=[vmem] * 4,
        out_specs=(vmem,) * 5,
        scratch_shapes=[
            pltpu.SemaphoreType.DMA((3,)),
            pltpu.SemaphoreType.DMA((3,)),
            pltpu.SemaphoreType.DMA((2, 2)),
            pltpu.SemaphoreType.DMA((2, 2)),
            pltpu.SemaphoreType.DMA((2, 3)),
            pltpu.SemaphoreType.DMA((3, 2)),
        ],
        compiler_params=pltpu.CompilerParams(
            collective_id=1, has_side_effects=True, vmem_limit_bytes=32 << 20
        ),
    )(tiles, grad, weight, edges)


def dot(a, b):
    return jnp.dot(a, b, preferred_element_type=jnp.float32)


def dot_lanes(a, b):
    return lax.dot_general(a, b, (((1,), (1,)), ((), ())), preferred_element_type=jnp.float32)


def group_kernel(
    known, full, grad, weight, side, cap, flags, mix, mix_turned, phases, columns, rows,
    merged, parts,
    phase, lr, taps, wide_weight, hidden, dpre, conv_sum,
):
    bf = jnp.bfloat16
    for ty in range(2):
        for j in range(4):
            lanes = pl.ds(256 * j, 256)
            picked = dot(full[ty, :, lanes], phases[:256]) + dot(full[2 + ty, :, lanes], phases[256:])
            out = pl.ds((4 * ty + j) * 128, 128)
            for q in range(4):
                phase[q, :, out] = picked[:, 128 * q : 128 * q + 128]
    zero = jnp.zeros((), bf)
    left = [jnp.where(known[0] >= 0, side[0, ty], zero) for ty in range(2)]
    right = [jnp.where(known[1] >= 0, side[1, ty], zero) for ty in range(2)]
    for ty in range(2):
        picked = dot(left[ty], columns[:128]) + dot(right[ty], columns[128:])
        for r in range(2):
            lr[r, :, pl.ds(512 * ty, 512)] = picked[:, 512 * r : 512 * r + 512]
    rim = jnp.zeros((128, 512), jnp.float32)
    for slot, entry in enumerate((2, 2, 3, 4)):
        rim += dot(jnp.where(known[entry] >= 0, cap[slot], zero), rows[128 * slot : 128 * slot + 128])
    lane = lax.broadcasted_iota(jnp.int32, (128, 1024), 1)
    first = (lane % 32) == 0
    final = (lane % 32) == 31
    narrow = lax.broadcasted_iota(jnp.int32, (128, 128), 1)
    for tx in range(4):
        for r in range(2):
            if tx == 0:
                base = jnp.where(first, lr[r], pltpu.roll(phase[2 * r + 1], 1, 1))
            elif tx == 1:
                base = phase[2 * r]
            elif tx == 2:
                base = phase[2 * r + 1]
            else:
                base = jnp.where(final, lr[r], pltpu.roll(phase[2 * r], 1023, 1))
            taps[pl.ds(((1 + r) * 4 + tx) * 128, 128), :] = base.astype(bf)
            corner = rim[:, 128 * tx : 128 * tx + 128]
            if r == 1:
                moved = pltpu.roll(base, 32, 1)
                at = pl.ds(tx * 128, 128)
                taps[at, 128:] = moved[:, 128:].astype(bf)
                taps[at, :128] = jnp.where(narrow < 32, corner, moved[:, :128]).astype(bf)
            else:
                moved = pltpu.roll(base, 992, 1)
                at = pl.ds((12 + tx) * 128, 128)
                taps[at, :896] = moved[:, :896].astype(bf)
                taps[at, 896:] = jnp.where(narrow >= 96, corner, moved[:, 896:]).astype(bf)
    for b in range(2):
        for i in range(3):
            blank = pl.ds((4 * i + (3 if b == 0 else 0)) * 128, 128)
            wide_weight[pl.ds(128 * b, 128), blank] = jnp.zeros((128, 128), bf)
            for j in range(3):
                for core in range(2):
                    wide_weight[pl.ds(128 * b + 64 * core, 64), pl.ds((4 * i + j + b) * 128, 128)] = (
                        weight[core, 3 * i + j]
                    )
    for a in range(2):
        at = pl.ds(256 * a, 256)
        pre = dot(wide_weight[...], taps[pl.ds(512 * a, 1536), :])
        kept = (jnp.maximum(pre, 0.0) * flags[...]).astype(bf)
        hidden[at, :] = kept
        upstream = dot(mix[at, :], grad[...])
        dpre[at, :] = jnp.where(kept.astype(jnp.float32) > 0, upstream, 0.0).astype(bf)
    for h in range(2):
        merged[h] = dot(mix_turned[pl.ds(128 * h, 128), :], hidden[...]).astype(bf)
    for i in range(3):
        strip = jnp.zeros((256, 512), jnp.float32)
        for a in range(2):
            strip += dot_lanes(dpre[pl.ds(256 * a, 256), :], taps[pl.ds(512 * (a + i), 512), :])
        for j in range(3):
            conv_sum[pl.ds((3 * i + j) * 128, 128), :] = (
                strip[:128, 128 * j : 128 * j + 128] + strip[128:, 128 * j + 128 : 128 * j + 256]
            )
    for piece in range(32):
        parts[piece, 0:36] = conv_sum[pl.ds(36 * piece, 36), :]
        parts[piece, 36:48] = jnp.zeros((12, 128), jnp.float32)
    mixed = dot_lanes(hidden[...], grad[...])
    for piece in range(32):
        parts[piece, 48:64] = mixed[16 * piece : 16 * piece + 16, :128]
        parts[piece, 64:80] = mixed[16 * piece : 16 * piece + 16, 128:]


def group_step(known, *arrays):
    bf, f32 = jnp.bfloat16, jnp.float32
    vmem = pl.BlockSpec(memory_space=pltpu.VMEM)
    return pl.pallas_call(
        group_kernel,
        name="group_step",
        out_shape=(
            jax.ShapeDtypeStruct((2, 128, 1024), bf),
            jax.ShapeDtypeStruct((32, 80, 128), f32),
        ),
        in_specs=[pl.BlockSpec(memory_space=pltpu.SMEM)] + [vmem] * len(arrays),
        out_specs=(vmem, vmem),
        scratch_shapes=[
            pltpu.VMEM((4, 128, 1024), f32),
            pltpu.VMEM((2, 128, 1024), f32),
            pltpu.VMEM((2048, 1024), bf),
            pltpu.VMEM((256, 1536), bf),
            pltpu.VMEM((512, 1024), bf),
            pltpu.VMEM((512, 1024), bf),
            pltpu.VMEM((1152, 128), f32),
        ],
        compiler_params=pltpu.CompilerParams(vmem_limit_bytes=48 << 20),
    )(known, *arrays)


def finish_kernel(
    n, part_ref, mine_ref, out_ref, merged_ref, near, held, recv,
    send_a, recv_a, send_b, recv_b, send_c, recv_c, chip_send, chip_recv,
):
    me = lax.axis_index("tile")
    core = lax.axis_index("chan")
    other = 1 - core
    barrier = pltpu.get_barrier_semaphore()

    def remote(src, dst, send_sem, recv_sem, row, column):
        copy = pltpu.make_async_remote_copy(
            src_ref=src,
            dst_ref=dst,
            send_sem=send_sem,
            recv_sem=recv_sem,
            device_id=(row, column),
            device_id_type=MESH,
        )
        copy.start()
        return copy

    for d in range(1, n):
        pl.semaphore_signal(
            barrier, inc=1, device_id=(lax.rem(me + d, n), core), device_id_type=MESH
        )
    pl.semaphore_signal(barrier, inc=1, device_id=(me, other), device_id_type=MESH)
    held[...] = part_ref[other].astype(held.dtype)
    pl.semaphore_wait(barrier, n)

    over = remote(held, near, chip_send.at[0], chip_recv.at[0], me, other)
    swap = remote(
        mine_ref.at[other], merged_ref.at[core], chip_send.at[1], chip_recv.at[1], me, other
    )
    merged_ref[core] = mine_ref[core]
    over.wait()
    held[...] = (part_ref[core] + near[...].astype(jnp.float32)).astype(held.dtype)

    scatter = []
    for d in range(1, n):
        peer = lax.rem(me + d, n)
        scatter.append(remote(held.at[peer], recv.at[d], send_a.at[d], recv_a.at[d], peer, core))
    total = part_ref[core, me] + near[me].astype(jnp.float32)
    for d in range(1, n):
        scatter[d - 1].wait_recv()
        total += recv[d].astype(jnp.float32)
    out_ref[core, me] = total.astype(out_ref.dtype)

    spread = []
    for d in range(1, n):
        own = out_ref.at[core, me]
        spread.append(remote(own, own, send_b.at[d], recv_b.at[d], lax.rem(me + d, n), core))
    for copy in spread:
        copy.wait_recv()
    crossing = remote(out_ref.at[core], out_ref.at[core], send_c.at[0], recv_c.at[0], me, other)
    for copy in scatter + spread:
        copy.wait_send()
    swap.wait()
    crossing.wait()


def finish(parts, mine, n):
    bf = jnp.bfloat16
    rows = parts.shape[2]
    vmem = pl.BlockSpec(memory_space=pltpu.VMEM)
    return pl.pallas_call(
        lambda *refs: finish_kernel(n, *refs),
        name="finish",
        out_shape=(
            jax.ShapeDtypeStruct((2, n, rows, LANES), bf),
            jax.ShapeDtypeStruct(mine.shape, bf),
        ),
        in_specs=[vmem] * 2,
        out_specs=(vmem, vmem),
        scratch_shapes=[pltpu.VMEM((n, rows, LANES), bf)] * 3
        + [pltpu.SemaphoreType.DMA((n,))] * 4
        + [pltpu.SemaphoreType.DMA((1,))] * 2
        + [pltpu.SemaphoreType.DMA((2,))] * 2,
        compiler_params=pltpu.CompilerParams(
            collective_id=2, has_side_effects=True, vmem_limit_bytes=32 << 20
        ),
    )(parts, mine)


def group_per_core(
    tile_features, conv_weight, merge_weight, tissue, group_tiles, neighbours, merged_grad
):
    bf = jnp.bfloat16
    n = lax.axis_size("tile")
    core = lax.axis_index("chan")
    local = group_tiles % tile_features.shape[0]
    order = local.reshape(2, 2, 2).transpose(0, 2, 1).reshape(-1)
    ordered = jnp.take(tile_features, order, axis=0)
    edges = jnp.einsum(
        "tcp,pe->tce", ordered, jnp.asarray(edge_picker()), preferred_element_type=jnp.float32
    ).astype(bf)
    full, grad_full, weight_full, side, cap = exchange(
        ordered.reshape(2, 4, 64, 1024),
        merged_grad,
        conv_weight.transpose(2, 3, 0, 1).reshape(9, 64, 128),
        edges.reshape(2, 2, 2, 64, 128),
        n,
    )
    known = lax.dynamic_index_in_dim(neighbours, core, 0, keepdims=False)
    upper = jnp.stack([known[2], known[3], known[0], known[4], known[5]])
    lower = jnp.stack([known[2], known[3], known[1], known[6], known[7]])
    entries = jnp.where(core == 1, upper, lower)
    mine = lax.dynamic_index_in_dim(local, core, 0, keepdims=False)
    flags = jnp.take(tissue, mine).astype(jnp.float32).reshape(2, 1, 2, 1)
    flags = jnp.broadcast_to(flags, (2, 16, 2, 16)).reshape(1, 1024)
    mix = merge_weight.transpose(1, 0, 2).reshape(512, 256)
    row_picks = lax.dynamic_index_in_dim(jnp.asarray(row_picker()), core, 0, keepdims=False)
    merged_all, parts = group_step(
        entries, full, grad_full, weight_full, side, cap, flags, mix, mix.T,
        jnp.asarray(phase_picker()), jnp.asarray(column_picker()), row_picks,
    )
    summed, merged = finish(parts.reshape(2, n, 80, LANES), merged_all, n)
    summed = summed.reshape(32, 80, LANES)
    grad_conv = summed[:, :36].reshape(3, 3, 128, 128).transpose(2, 3, 0, 1).astype(jnp.float32)
    grad_merge = (
        summed[:, 48:].reshape(4, 8, 2, 16, LANES).transpose(0, 1, 3, 2, 4)
        .reshape(4, 128, 256).transpose(1, 0, 2).astype(jnp.float32)
    )
    return merged, grad_conv, grad_merge


def solution(mesh):
    placed = (
        P("tile", "chan", None),
        P("chan", None, None, None),
        P(),
        P("tile"),
        P("tile", None),
        P("tile", None),
        P("tile", "chan", None),
    )
    pairs = mesh.shape["chan"] == 2 and mesh.shape["tile"] == 16
    return jax.shard_map(
        group_per_core if pairs else shards,
        mesh=mesh,
        in_specs=placed,
        out_specs=(P("tile", "chan", None), P(), P()),
        check_vma=False,
    )
```

```python
import jax
import ml_dtypes
import numpy as np
import jax.numpy as jnp
from jax import lax
from jax.experimental import pallas as pl
from jax.experimental.pallas import tpu as pltpu
from jax.sharding import PartitionSpec as P

PIX = 32


OPPOSITE = (1, 0, 3, 2, 7, 6, 5, 4)
ROW_STEPS = (-1, 1, 0, 0, -1, -1, 1, 1)
COLUMN_STEPS = (0, 0, -1, 1, -1, 1, -1, 1)


def passed_along(block, axis, distance):
    devices = range(lax.axis_size(axis))
    route = [((i - distance) % len(devices), i) for i in devices]
    return lax.ppermute(block, axis, route)


def boundary(picture):
    top_row = picture[:, :, 0, :]
    bottom_row = picture[:, :, -1, :]
    left_column = picture[:, :, :, 0]
    right_column = picture[:, :, :, -1]
    return jnp.stack(
        [top_row, bottom_row, left_column, right_column, top_row, top_row, bottom_row, bottom_row],
        axis=1,
    )


def assemble(tile_rows, local_ids, width):
    number = local_ids.shape[0]
    channels = tile_rows.shape[1]
    picked = jnp.take(tile_rows, local_ids.reshape(-1), axis=0)
    picked = picked.reshape(number, 2, 2, channels, width, width)
    return picked.transpose(0, 3, 1, 4, 2, 5).reshape(number, channels, 2 * width, 2 * width)


def framed(picture, rim_cells):
    extent = picture.shape[2]
    upper = jnp.concatenate(
        [rim_cells[:, 4, :, extent - 1 :], rim_cells[:, 0], rim_cells[:, 5, :, :1]], axis=2
    )
    lower = jnp.concatenate(
        [rim_cells[:, 6, :, extent - 1 :], rim_cells[:, 1], rim_cells[:, 7, :, :1]], axis=2
    )
    middle = jnp.concatenate(
        [rim_cells[:, 2][..., None], picture, rim_cells[:, 3][..., None]], axis=3
    )
    return jnp.concatenate([upper[:, :, None, :], middle, lower[:, :, None, :]], axis=2)


def tissue_map(tissue_rows, width):
    number = tissue_rows.shape[0]
    layout = tissue_rows.reshape(number, 2, 1, 2, 1)
    return jnp.broadcast_to(layout, (number, 2, width, 2, width)).reshape(
        number, 2 * width, 2 * width
    )


def to_blocks(hidden, width):
    number, channels = (hidden.shape[0], hidden.shape[1])
    shaped = hidden.reshape(number, channels, width, 2, width, 2)
    return shaped.transpose(0, 3, 5, 1, 2, 4).reshape(number, 4, channels, width * width)


def from_blocks(blocks, width):
    number, channels = (blocks.shape[0], blocks.shape[2])
    shaped = blocks.reshape(number, 2, 2, channels, width, width)
    return shaped.transpose(0, 3, 4, 1, 5, 2).reshape(number, channels, 2 * width, 2 * width)


MESH = pl.DeviceIdType.MESH
LANES = 128


def total_kernel(n, nc, part_ref, out_ref, recv, send_a, recv_a, send_b, recv_b, send_c, recv_c):
    me = lax.axis_index("tile")
    core = lax.axis_index("chan")
    barrier = pltpu.get_barrier_semaphore()
    for d in range(1, n):
        pl.semaphore_signal(
            barrier, inc=1, device_id=(lax.rem(me + d, n), core), device_id_type=MESH
        )
    for d in range(1, nc):
        pl.semaphore_signal(
            barrier, inc=1, device_id=(me, lax.rem(core + d, nc)), device_id_type=MESH
        )
    pl.semaphore_wait(barrier, n - 1 + nc - 1)

    scatter = []
    for d in range(1, n):
        peer = lax.rem(me + d, n)
        copy = pltpu.make_async_remote_copy(
            src_ref=part_ref.at[peer],
            dst_ref=recv.at[d],
            send_sem=send_a.at[d],
            recv_sem=recv_a.at[d],
            device_id=(peer, core),
            device_id_type=MESH,
        )
        copy.start()
        scatter.append(copy)
    total = part_ref[me].astype(jnp.float32)
    for d in range(1, n):
        scatter[d - 1].wait_recv()
        total += recv[d].astype(jnp.float32)
    out_ref[core, me] = total.astype(out_ref.dtype)

    spread = []
    for d in range(1, n):
        copy = pltpu.make_async_remote_copy(
            src_ref=out_ref.at[core, me],
            dst_ref=out_ref.at[core, me],
            send_sem=send_b.at[d],
            recv_sem=recv_b.at[d],
            device_id=(lax.rem(me + d, n), core),
            device_id_type=MESH,
        )
        copy.start()
        spread.append(copy)
    for copy in spread:
        copy.wait_recv()
    crossing = []
    for d in range(1, nc):
        copy = pltpu.make_async_remote_copy(
            src_ref=out_ref.at[core],
            dst_ref=out_ref.at[core],
            send_sem=send_c.at[d],
            recv_sem=recv_c.at[d],
            device_id=(me, lax.rem(core + d, nc)),
            device_id_type=MESH,
        )
        copy.start()
        crossing.append(copy)
    for copy in scatter + spread:
        copy.wait_send()
    for copy in crossing:
        copy.wait()


def totals(parts, n, nc):
    rows = parts.shape[1]
    return pl.pallas_call(
        lambda *refs: total_kernel(n, nc, *refs),
        name="weight_totals",
        out_shape=jax.ShapeDtypeStruct((nc, n, rows, LANES), parts.dtype),
        in_specs=[pl.BlockSpec(memory_space=pltpu.VMEM)],
        out_specs=pl.BlockSpec(memory_space=pltpu.VMEM),
        scratch_shapes=[pltpu.VMEM((n, rows, LANES), parts.dtype)]
        + [pltpu.SemaphoreType.DMA((n,))] * 4
        + [pltpu.SemaphoreType.DMA((nc,))] * 2,
        compiler_params=pltpu.CompilerParams(collective_id=0, has_side_effects=True),
    )(parts)


def shards(tile_features, conv_weight, merge_weight, tissue, group_tiles, neighbours, merged_grad):
    chan_index = lax.axis_index("chan")
    local_groups = neighbours.shape[0]
    local_tiles = tile_features.shape[0]
    own_chan = tile_features.shape[1]
    own_merged = merged_grad.shape[1]
    extent = 2 * PIX
    local_ids = group_tiles % local_tiles
    own_picture = assemble(tile_features, local_ids, PIX)
    own_edges = boundary(own_picture)
    sides = []
    for direction in range(8):
        row_step = ROW_STEPS[direction]
        device_step = COLUMN_STEPS[direction] + 4 * row_step
        sending = own_edges[:, OPPOSITE[direction]]
        arrived = passed_along(sending, "tile", -device_step)
        blank = jnp.zeros((1, own_chan, extent), jnp.bfloat16)
        if row_step == 1:
            aligned = jnp.concatenate([arrived[1:], blank], axis=0)
        elif row_step == -1:
            aligned = jnp.concatenate([blank, arrived[:-1]], axis=0)
        else:
            aligned = arrived
        present_rows = (neighbours[:, direction] >= 0)[:, None, None]
        sides.append(jnp.where(present_rows, aligned, jnp.zeros((), jnp.bfloat16)))
    rim_flat = jnp.stack(sides, axis=2).reshape(local_groups, own_chan, 8 * extent)
    all_tiles, all_rims = (
        lax.all_gather(tile_features, "chan", axis=1, tiled=True),
        lax.all_gather(rim_flat, "chan", axis=1, tiled=True),
    )
    channels_all = all_tiles.shape[1]
    rim_cells = all_rims.reshape(local_groups, channels_all, 8, extent).transpose(0, 2, 1, 3)
    padded = framed(assemble(all_tiles, local_ids, PIX), rim_cells)
    conv_out = lax.conv_general_dilated(
        padded,
        conv_weight,
        (1, 1),
        "VALID",
        dimension_numbers=("NCHW", "OIHW", "NCHW"),
        preferred_element_type=jnp.float32,
    )
    tissue_rows = (
        jnp.take(tissue, local_ids.reshape(-1)).reshape(local_groups, 4).astype(jnp.float32)
    )
    hidden = (jnp.maximum(conv_out, 0.0) * tissue_map(tissue_rows, PIX)[:, None]).astype(
        jnp.bfloat16
    )
    hidden_blocks = to_blocks(hidden, PIX)
    merge_rows = lax.dynamic_slice_in_dim(merge_weight, chan_index * own_chan, own_chan, 0)
    every_block = lax.all_gather(hidden_blocks, "chan", axis=2, tiled=True)
    merge_columns = lax.dynamic_slice_in_dim(merge_weight, chan_index * own_merged, own_merged, 2)
    merged = jnp.einsum(
        "ckm,gkcq->gmq", merge_columns, every_block, preferred_element_type=jnp.float32
    ).astype(jnp.bfloat16)
    upstream = lax.all_gather(merged_grad, "chan", axis=1, tiled=True)
    grad_hidden = from_blocks(
        jnp.einsum("ckm,gmq->gkcq", merge_rows, upstream, preferred_element_type=jnp.float32), PIX
    )
    grad_pre = jnp.where(hidden > 0, grad_hidden, 0.0).astype(jnp.bfloat16)
    merge_term = jnp.einsum(
        "gmq,gkcq->ckm", upstream, hidden_blocks, preferred_element_type=jnp.float32
    )
    conv_term = lax.conv_general_dilated(
        padded,
        grad_pre,
        (1, 1),
        "VALID",
        dimension_numbers=("CNHW", "IOHW", "NCHW"),
        preferred_element_type=jnp.float32,
    )
    conv_term = conv_term.transpose(1, 0, 2, 3)
    n = lax.axis_size("tile")
    nc = lax.axis_size("chan")
    conv_rows = conv_term.transpose(2, 3, 0, 1).reshape(-1, LANES)
    merge_rows_part = merge_term.reshape(-1, LANES)
    stacked = jnp.concatenate([conv_rows, merge_rows_part], axis=0).astype(jnp.bfloat16)
    used = stacked.shape[0]
    rows = -(-used // (16 * n)) * 16
    parts = jnp.pad(stacked, ((0, rows * n - used), (0, 0))).reshape(n, rows, LANES)
    summed = totals(parts, n, nc).reshape(nc, n * rows, LANES)
    conv_count = conv_rows.shape[0]
    grad_conv = (
        summed[:, :conv_count]
        .reshape(nc, 3, 3, own_chan, channels_all)
        .transpose(0, 3, 4, 1, 2)
        .reshape(channels_all, channels_all, 3, 3)
        .astype(jnp.float32)
    )
    grad_merge = (
        summed[:, conv_count:used].reshape(merge_weight.shape).astype(jnp.float32)
    )
    return (merged, grad_conv, grad_merge)


def edge_picker():
    picks = np.zeros((PIX * PIX, 4 * PIX), np.float32)
    for i in range(PIX):
        picks[i, i] = 1
        picks[(PIX - 1) * PIX + i, PIX + i] = 1
        picks[i * PIX, 2 * PIX + i] = 1
        picks[i * PIX + PIX - 1, 3 * PIX + i] = 1
    return picks.astype(ml_dtypes.bfloat16)


def phase_picker():
    picks = np.zeros((2, 8, PIX, 2, 2, 4, PIX), np.float32)
    for side in range(2):
        for row in range(8):
            for x in range(PIX):
                picks[side, row, x, row % 2, x % 2, row // 2, 16 * side + x // 2] = 1
    return picks.reshape(512, 512).astype(ml_dtypes.bfloat16)


def column_picker():
    picks = np.zeros((2, 4 * PIX, 2, 16, PIX), np.float32)
    for r in range(2):
        for y in range(16):
            picks[0, 3 * PIX + 2 * y + r, r, y, 0] = 1
            picks[1, 2 * PIX + 2 * y + r, r, y, PIX - 1] = 1
    return picks.reshape(256, 1024).astype(ml_dtypes.bfloat16)


def row_picker():
    picks = np.zeros((2, 4, 4 * PIX, 4, 128), np.float32)
    for core in range(2):
        base = PIX * core
        for t in range(4):
            for x in range(PIX):
                at = 2 * x + t
                out = x if core == 1 else 96 + x
                if at == 0:
                    slot, lane = 2, base + PIX - 1
                elif at == 65:
                    slot, lane = 3, base
                else:
                    slot, lane = (at - 1) // PIX, base + (at - 1) % PIX
                picks[core, slot, lane, t, out] = 1
    return picks.reshape(2, 512, 512).astype(ml_dtypes.bfloat16)


def exchange_kernel(
    n, ids, stored, grad, weight, picks, full, grad_full, weight_full, side, cap,
    tiles, sides, caps, corners, send_own, recv_own, send_side, recv_side, send_cap, recv_cap,
):
    p = lax.axis_index("tile")
    k = lax.axis_index("chan")
    other = 1 - k
    toward = 1 - 2 * k
    barrier = pltpu.get_barrier_semaphore()

    def at(step):
        return lax.rem(p + step + n, n)

    def greet(row, core):
        pl.semaphore_signal(barrier, inc=1, device_id=(row, core), device_id_type=MESH)

    greet(p, other)
    for core in range(2):
        for step in (-1, 1):
            greet(at(step), core)
        for step in (3, 4, 5):
            greet(at(toward * step), core)
    count = stored.shape[0]
    for g in range(2):
        for column in range(2):
            for row in range(2):
                tiles[g, 2 * column + row] = stored[lax.rem(ids[g, 2 * row + column], count)]
    edge = dot(tiles[...].reshape(512, 1024), picks[...])
    lane = lax.broadcasted_iota(jnp.int32, (64, 128), 1)

    def edge_of(g, column, row):
        start = 64 * (4 * g + 2 * column + row)
        return edge[start : start + 64]

    bf = jnp.bfloat16
    for g in range(2):
        sides[g, 0] = jnp.where(
            lane < 96, edge_of(g, 0, 0), pltpu.roll(edge_of(g, 0, 1), 32, 1)
        ).astype(bf)
        sides[g, 1] = jnp.where(
            lane >= 96, edge_of(g, 1, 0), pltpu.roll(edge_of(g, 1, 1), 96, 1)
        ).astype(bf)
    for target in range(2):
        g = 1 - target
        caps[target] = jnp.where(
            lane < 32 + 32 * target,
            edge_of(g, 0, target),
            pltpu.roll(edge_of(g, 1, target), 32, 1),
        ).astype(bf)
        for column in range(2):
            corners[target, column] = edge_of(g, column, target).astype(bf)
    pl.semaphore_wait(barrier, 11)

    def send(src, dst, send_sem, recv_sem, row, core):
        copy = pltpu.make_async_remote_copy(
            src_ref=src,
            dst_ref=dst,
            send_sem=send_sem,
            recv_sem=recv_sem,
            device_id=(row, core),
            device_id_type=MESH,
        )
        copy.start()
        return copy

    half = pl.ds(pl.multiple_of(64 * k, 64), 64)
    wide = pl.ds(pl.multiple_of(128 * k, 128), 128)
    copies = []
    for g in range(2):
        for s, step in ((0, 1), (1, -1)):
            copies.append(
                send(
                    sides.at[g, 1 - s], side.at[s, half],
                    send_side.at[g, s], recv_side.at[s, k], at(step), g,
                )
            )
    for target, sign in ((1, 1), (0, -1)):
        copies.append(
            send(
                caps.at[target], cap.at[0, half],
                send_cap.at[target, 0], recv_cap.at[0, k], at(4 * sign), target,
            )
        )
        for slot, step, column in ((1, 5 if sign > 0 else -3, 1), (2, 3 if sign > 0 else -5, 0)):
            copies.append(
                send(
                    corners.at[target, column], cap.at[slot, half],
                    send_cap.at[target, slot], recv_cap.at[slot, k], at(step), target,
                )
            )
    copies.append(send(tiles.at[other], full.at[:, half], send_own.at[0], recv_own.at[0], p, other))
    copies.append(send(grad.at[other], grad_full.at[wide], send_own.at[1], recv_own.at[1], p, other))
    copies.append(send(weight, weight_full.at[k], send_own.at[2], recv_own.at[2], p, other))
    full[:, half] = tiles[k]
    grad_full[wide] = grad[k]
    weight_full[k] = weight[...]
    for copy in copies:
        copy.wait_send()
    copies[-1].wait_recv()
    copies[-2].wait_recv()
    copies[-3].wait_recv()

    def arrived(dst, recv_sem):
        pltpu.make_async_remote_copy(
            src_ref=dst,
            dst_ref=dst,
            send_sem=send_own.at[0],
            recv_sem=recv_sem,
            device_id=(p, other),
            device_id_type=MESH,
        ).wait_recv()

    for core in range(2):
        part = pl.ds(64 * core, 64)
        for s in range(2):
            arrived(side.at[s, part], recv_side.at[s, core])
        for slot in range(3):
            arrived(cap.at[slot, part], recv_cap.at[slot, core])


def exchange(ids, tiles, grad, weight, picks, n):
    bf = jnp.bfloat16
    vmem = pl.BlockSpec(memory_space=pltpu.VMEM)
    return pl.pallas_call(
        lambda *refs: exchange_kernel(n, *refs),
        name="exchange",
        out_shape=(
            jax.ShapeDtypeStruct((4, 128, 1024), bf),
            jax.ShapeDtypeStruct((256, 1024), bf),
            jax.ShapeDtypeStruct((2, 9, 64, 128), bf),
            jax.ShapeDtypeStruct((2, 128, 128), bf),
            jax.ShapeDtypeStruct((3, 128, 128), bf),
        ),
        in_specs=[pl.BlockSpec(memory_space=pltpu.SMEM)] + [vmem] * 4,
        out_specs=(vmem,) * 5,
        scratch_shapes=[
            pltpu.VMEM((2, 4, 64, 1024), bf),
            pltpu.VMEM((2, 2, 64, 128), bf),
            pltpu.VMEM((2, 64, 128), bf),
            pltpu.VMEM((2, 2, 64, 128), bf),
            pltpu.SemaphoreType.DMA((3,)),
            pltpu.SemaphoreType.DMA((3,)),
            pltpu.SemaphoreType.DMA((2, 2)),
            pltpu.SemaphoreType.DMA((2, 2)),
            pltpu.SemaphoreType.DMA((2, 3)),
            pltpu.SemaphoreType.DMA((3, 2)),
        ],
        compiler_params=pltpu.CompilerParams(
            collective_id=1, has_side_effects=True, vmem_limit_bytes=32 << 20
        ),
    )(ids, tiles, grad, weight, picks)


def dot(a, b):
    return jnp.dot(a, b, preferred_element_type=jnp.float32)


def dot_lanes(a, b):
    return lax.dot_general(a, b, (((1,), (1,)), ((), ())), preferred_element_type=jnp.float32)


def group_kernel(
    near_groups, ids, tissue, full, grad, weight, side, cap, mix, mix_turned, phases, columns, rows,
    merged, parts,
    phase, lr, taps, wide_weight, hidden, dpre, conv_sum,
):
    bf = jnp.bfloat16
    core = lax.axis_index("chan")
    count = tissue.shape[0]
    entry_of = (2, 3, core * -1 + 1, core * -2 + 6, core * -2 + 7)
    known = [near_groups[core, entry] for entry in entry_of]
    kinds = [tissue[lax.rem(ids[core, t], count)].astype(jnp.float32) for t in range(4)]
    spot = lax.broadcasted_iota(jnp.int32, (1, 1024), 1)
    east = (spot % 32) >= 16
    flags = jnp.where(
        spot >= 512, jnp.where(east, kinds[3], kinds[2]), jnp.where(east, kinds[1], kinds[0])
    )
    for ty in range(2):
        for j in range(4):
            lanes = pl.ds(256 * j, 256)
            picked = dot(full[ty, :, lanes], phases[:256]) + dot(full[2 + ty, :, lanes], phases[256:])
            out = pl.ds((4 * ty + j) * 128, 128)
            for q in range(4):
                phase[q, :, out] = picked[:, 128 * q : 128 * q + 128]
    zero = jnp.zeros((), bf)
    blank_side = jnp.zeros((), jnp.float32)
    near_left = jnp.where(known[0] >= 0, side[0].astype(jnp.float32), blank_side)
    near_right = jnp.where(known[1] >= 0, side[1].astype(jnp.float32), blank_side)
    near_cap = jnp.where(known[2] >= 0, cap[0].astype(jnp.float32), blank_side)
    left = [near_left.astype(bf), pltpu.roll(near_left, 32, 1).astype(bf)]
    right = [near_right.astype(bf), pltpu.roll(near_right, 96, 1).astype(bf)]
    for ty in range(2):
        picked = dot(left[ty], columns[:128]) + dot(right[ty], columns[128:])
        for r in range(2):
            lr[r, :, pl.ds(512 * ty, 512)] = picked[:, 512 * r : 512 * r + 512]
    rim = jnp.zeros((128, 512), jnp.float32)
    row_sources = (
        near_cap.astype(bf),
        pltpu.roll(near_cap, 96, 1).astype(bf),
        jnp.where(known[3] >= 0, cap[1], zero),
        jnp.where(known[4] >= 0, cap[2], zero),
    )
    for slot, source in enumerate(row_sources):
        rim += dot(source, rows[core, pl.ds(128 * slot, 128), :])
    lane = lax.broadcasted_iota(jnp.int32, (128, 1024), 1)
    first = (lane % 32) == 0
    final = (lane % 32) == 31
    narrow = lax.broadcasted_iota(jnp.int32, (128, 128), 1)
    for tx in range(4):
        for r in range(2):
            if tx == 0:
                base = jnp.where(first, lr[r], pltpu.roll(phase[2 * r + 1], 1, 1))
            elif tx == 1:
                base = phase[2 * r]
            elif tx == 2:
                base = phase[2 * r + 1]
            else:
                base = jnp.where(final, lr[r], pltpu.roll(phase[2 * r], 1023, 1))
            taps[pl.ds(((1 + r) * 4 + tx) * 128, 128), :] = base.astype(bf)
            corner = rim[:, 128 * tx : 128 * tx + 128]
            if r == 1:
                moved = pltpu.roll(base, 32, 1)
                at = pl.ds(tx * 128, 128)
                taps[at, 128:] = moved[:, 128:].astype(bf)
                taps[at, :128] = jnp.where(narrow < 32, corner, moved[:, :128]).astype(bf)
            else:
                moved = pltpu.roll(base, 992, 1)
                at = pl.ds((12 + tx) * 128, 128)
                taps[at, :896] = moved[:, :896].astype(bf)
                taps[at, 896:] = jnp.where(narrow >= 96, corner, moved[:, 896:]).astype(bf)
    for b in range(2):
        for i in range(3):
            blank = pl.ds((4 * i + (3 if b == 0 else 0)) * 128, 128)
            wide_weight[pl.ds(128 * b, 128), blank] = jnp.zeros((128, 128), bf)
            for j in range(3):
                for core in range(2):
                    wide_weight[pl.ds(128 * b + 64 * core, 64), pl.ds((4 * i + j + b) * 128, 128)] = (
                        weight[core, 3 * i + j]
                    )
    for a in range(2):
        at = pl.ds(256 * a, 256)
        pre = dot(wide_weight[...], taps[pl.ds(512 * a, 1536), :])
        kept = (jnp.maximum(pre, 0.0) * flags).astype(bf)
        hidden[at, :] = kept
        upstream = dot(mix[at, :], grad[...])
        dpre[at, :] = jnp.where(kept.astype(jnp.float32) > 0, upstream, 0.0).astype(bf)
    for h in range(2):
        merged[h] = dot(mix_turned[pl.ds(128 * h, 128), :], hidden[...]).astype(bf)
    for i in range(3):
        strip = jnp.zeros((256, 512), jnp.float32)
        for a in range(2):
            strip += dot_lanes(dpre[pl.ds(256 * a, 256), :], taps[pl.ds(512 * (a + i), 512), :])
        for j in range(3):
            conv_sum[pl.ds((3 * i + j) * 128, 128), :] = (
                strip[:128, 128 * j : 128 * j + 128] + strip[128:, 128 * j + 128 : 128 * j + 256]
            )
    for piece in range(32):
        parts[piece, 0:36] = conv_sum[pl.ds(36 * piece, 36), :]
        parts[piece, 36:48] = jnp.zeros((12, 128), jnp.float32)
    mixed = dot_lanes(hidden[...], grad[...])
    for piece in range(32):
        parts[piece, 48:64] = mixed[16 * piece : 16 * piece + 16, :128]
        parts[piece, 64:80] = mixed[16 * piece : 16 * piece + 16, 128:]


def group_step(near_groups, ids, tissue, *arrays):
    bf, f32 = jnp.bfloat16, jnp.float32
    vmem = pl.BlockSpec(memory_space=pltpu.VMEM)
    return pl.pallas_call(
        group_kernel,
        name="group_step",
        out_shape=(
            jax.ShapeDtypeStruct((2, 128, 1024), bf),
            jax.ShapeDtypeStruct((32, 80, 128), f32),
        ),
        in_specs=[pl.BlockSpec(memory_space=pltpu.SMEM)] * 3 + [vmem] * len(arrays),
        out_specs=(vmem, vmem),
        scratch_shapes=[
            pltpu.VMEM((4, 128, 1024), f32),
            pltpu.VMEM((2, 128, 1024), f32),
            pltpu.VMEM((2048, 1024), bf),
            pltpu.VMEM((256, 1536), bf),
            pltpu.VMEM((512, 1024), bf),
            pltpu.VMEM((512, 1024), bf),
            pltpu.VMEM((1152, 128), f32),
        ],
        compiler_params=pltpu.CompilerParams(vmem_limit_bytes=48 << 20),
    )(near_groups, ids, tissue, *arrays)


def finish_kernel(
    n, part_ref, mine_ref, conv_ref, mix_ref, merged_ref, out_ref, near, held, recv,
    send_a, recv_a, send_b, recv_b, send_c, recv_c, chip_send, chip_recv,
):
    me = lax.axis_index("tile")
    core = lax.axis_index("chan")
    other = 1 - core
    barrier = pltpu.get_barrier_semaphore()

    def remote(src, dst, send_sem, recv_sem, row, column):
        copy = pltpu.make_async_remote_copy(
            src_ref=src,
            dst_ref=dst,
            send_sem=send_sem,
            recv_sem=recv_sem,
            device_id=(row, column),
            device_id_type=MESH,
        )
        copy.start()
        return copy

    for d in range(1, n):
        pl.semaphore_signal(
            barrier, inc=1, device_id=(lax.rem(me + d, n), core), device_id_type=MESH
        )
    pl.semaphore_signal(barrier, inc=1, device_id=(me, other), device_id_type=MESH)
    held[...] = part_ref[other].astype(held.dtype)
    pl.semaphore_wait(barrier, n)

    over = remote(held, near, chip_send.at[0], chip_recv.at[0], me, other)
    swap = remote(
        mine_ref.at[other], merged_ref.at[core], chip_send.at[1], chip_recv.at[1], me, other
    )
    merged_ref[core] = mine_ref[core]
    over.wait()
    held[...] = (part_ref[core] + near[...].astype(jnp.float32)).astype(held.dtype)

    scatter = []
    for d in range(1, n):
        peer = lax.rem(me + d, n)
        scatter.append(remote(held.at[peer], recv.at[d], send_a.at[d], recv_a.at[d], peer, core))
    total = part_ref[core, me] + near[me].astype(jnp.float32)
    for d in range(1, n):
        scatter[d - 1].wait_recv()
        total += recv[d].astype(jnp.float32)
    out_ref[core, me] = total.astype(out_ref.dtype)

    spread = []
    for d in range(1, n):
        own = out_ref.at[core, me]
        spread.append(remote(own, own, send_b.at[d], recv_b.at[d], lax.rem(me + d, n), core))
    own = out_ref.at[core, me]
    crossing = [remote(own, own, send_c.at[0], recv_c.at[0], me, other)]
    for d in range(1, n):
        spread[d - 1].wait_recv()
        piece = out_ref.at[core, lax.rem(me + n - d, n)]
        crossing.append(remote(piece, piece, send_c.at[d], recv_c.at[d], me, other))
    for copy in scatter + spread:
        copy.wait_send()
    swap.wait()
    for copy in crossing:
        copy.wait()
    for piece in range(32):
        block = out_ref[piece // n, piece % n].astype(jnp.float32)
        conv_ref[pl.ds(36 * piece, 36), :] = block[:36]
        mix_ref[pl.ds(16 * piece, 16), :128] = block[48:64]
        mix_ref[pl.ds(16 * piece, 16), 128:] = block[64:]


def finish(parts, mine, n):
    bf = jnp.bfloat16
    rows = parts.shape[2]
    vmem = pl.BlockSpec(memory_space=pltpu.VMEM)
    return pl.pallas_call(
        lambda *refs: finish_kernel(n, *refs),
        name="finish",
        out_shape=(
            jax.ShapeDtypeStruct((1152, LANES), jnp.float32),
            jax.ShapeDtypeStruct((512, 2 * LANES), jnp.float32),
            jax.ShapeDtypeStruct(mine.shape, bf),
        ),
        in_specs=[vmem] * 2,
        out_specs=(vmem, vmem, vmem),
        scratch_shapes=[pltpu.VMEM((2, n, rows, LANES), bf)]
        + [pltpu.VMEM((n, rows, LANES), bf)] * 3
        + [pltpu.SemaphoreType.DMA((n,))] * 6
        + [pltpu.SemaphoreType.DMA((2,))] * 2,
        compiler_params=pltpu.CompilerParams(
            collective_id=2, has_side_effects=True, vmem_limit_bytes=32 << 20
        ),
    )(parts, mine)


def group_per_core(
    tile_features, conv_weight, merge_weight, tissue, group_tiles, neighbours, merged_grad
):
    n = lax.axis_size("tile")
    full, grad_full, weight_full, side, cap = exchange(
        group_tiles,
        tile_features,
        merged_grad,
        conv_weight.transpose(2, 3, 0, 1).reshape(9, 64, 128),
        jnp.asarray(edge_picker()),
        n,
    )
    mix = merge_weight.transpose(1, 0, 2).reshape(512, 256)
    merged_all, parts = group_step(
        neighbours, group_tiles, tissue, full, grad_full, weight_full, side, cap, mix, mix.T,
        jnp.asarray(phase_picker()), jnp.asarray(column_picker()), jnp.asarray(row_picker()),
    )
    summed_conv, summed_mix, merged = finish(parts.reshape(2, n, 80, LANES), merged_all, n)
    grad_conv = summed_conv.reshape(3, 3, 128, 128).transpose(2, 3, 0, 1)
    grad_merge = summed_mix.reshape(4, 128, 256).transpose(1, 0, 2)
    return merged, grad_conv, grad_merge


def solution(mesh):
    placed = (
        P("tile", "chan", None),
        P("chan", None, None, None),
        P(),
        P("tile"),
        P("tile", None),
        P("tile", None),
        P("tile", "chan", None),
    )
    pairs = mesh.shape["chan"] == 2 and mesh.shape["tile"] == 16
    return jax.shard_map(
        group_per_core if pairs else shards,
        mesh=mesh,
        in_specs=placed,
        out_specs=(P("tile", "chan", None), P(), P()),
        check_vma=False,
    )
```

```python
import jax
import ml_dtypes
import numpy as np
import jax.numpy as jnp
from jax import lax
from jax.experimental import pallas as pl
from jax.experimental.pallas import tpu as pltpu
from jax.sharding import PartitionSpec as P

PIX = 32


OPPOSITE = (1, 0, 3, 2, 7, 6, 5, 4)
ROW_STEPS = (-1, 1, 0, 0, -1, -1, 1, 1)
COLUMN_STEPS = (0, 0, -1, 1, -1, 1, -1, 1)


def passed_along(block, axis, distance):
    devices = range(lax.axis_size(axis))
    route = [((i - distance) % len(devices), i) for i in devices]
    return lax.ppermute(block, axis, route)


def boundary(picture):
    top_row = picture[:, :, 0, :]
    bottom_row = picture[:, :, -1, :]
    left_column = picture[:, :, :, 0]
    right_column = picture[:, :, :, -1]
    return jnp.stack(
        [top_row, bottom_row, left_column, right_column, top_row, top_row, bottom_row, bottom_row],
        axis=1,
    )


def assemble(tile_rows, local_ids, width):
    number = local_ids.shape[0]
    channels = tile_rows.shape[1]
    picked = jnp.take(tile_rows, local_ids.reshape(-1), axis=0)
    picked = picked.reshape(number, 2, 2, channels, width, width)
    return picked.transpose(0, 3, 1, 4, 2, 5).reshape(number, channels, 2 * width, 2 * width)


def framed(picture, rim_cells):
    extent = picture.shape[2]
    upper = jnp.concatenate(
        [rim_cells[:, 4, :, extent - 1 :], rim_cells[:, 0], rim_cells[:, 5, :, :1]], axis=2
    )
    lower = jnp.concatenate(
        [rim_cells[:, 6, :, extent - 1 :], rim_cells[:, 1], rim_cells[:, 7, :, :1]], axis=2
    )
    middle = jnp.concatenate(
        [rim_cells[:, 2][..., None], picture, rim_cells[:, 3][..., None]], axis=3
    )
    return jnp.concatenate([upper[:, :, None, :], middle, lower[:, :, None, :]], axis=2)


def tissue_map(tissue_rows, width):
    number = tissue_rows.shape[0]
    layout = tissue_rows.reshape(number, 2, 1, 2, 1)
    return jnp.broadcast_to(layout, (number, 2, width, 2, width)).reshape(
        number, 2 * width, 2 * width
    )


def to_blocks(hidden, width):
    number, channels = (hidden.shape[0], hidden.shape[1])
    shaped = hidden.reshape(number, channels, width, 2, width, 2)
    return shaped.transpose(0, 3, 5, 1, 2, 4).reshape(number, 4, channels, width * width)


def from_blocks(blocks, width):
    number, channels = (blocks.shape[0], blocks.shape[2])
    shaped = blocks.reshape(number, 2, 2, channels, width, width)
    return shaped.transpose(0, 3, 4, 1, 5, 2).reshape(number, channels, 2 * width, 2 * width)


MESH = pl.DeviceIdType.MESH
LANES = 128


def total_kernel(n, nc, part_ref, out_ref, recv, send_a, recv_a, send_b, recv_b, send_c, recv_c):
    me = lax.axis_index("tile")
    core = lax.axis_index("chan")
    barrier = pltpu.get_barrier_semaphore()
    for d in range(1, n):
        pl.semaphore_signal(
            barrier, inc=1, device_id=(lax.rem(me + d, n), core), device_id_type=MESH
        )
    for d in range(1, nc):
        pl.semaphore_signal(
            barrier, inc=1, device_id=(me, lax.rem(core + d, nc)), device_id_type=MESH
        )
    pl.semaphore_wait(barrier, n - 1 + nc - 1)

    scatter = []
    for d in range(1, n):
        peer = lax.rem(me + d, n)
        copy = pltpu.make_async_remote_copy(
            src_ref=part_ref.at[peer],
            dst_ref=recv.at[d],
            send_sem=send_a.at[d],
            recv_sem=recv_a.at[d],
            device_id=(peer, core),
            device_id_type=MESH,
        )
        copy.start()
        scatter.append(copy)
    total = part_ref[me].astype(jnp.float32)
    for d in range(1, n):
        scatter[d - 1].wait_recv()
        total += recv[d].astype(jnp.float32)
    out_ref[core, me] = total.astype(out_ref.dtype)

    spread = []
    for d in range(1, n):
        copy = pltpu.make_async_remote_copy(
            src_ref=out_ref.at[core, me],
            dst_ref=out_ref.at[core, me],
            send_sem=send_b.at[d],
            recv_sem=recv_b.at[d],
            device_id=(lax.rem(me + d, n), core),
            device_id_type=MESH,
        )
        copy.start()
        spread.append(copy)
    for copy in spread:
        copy.wait_recv()
    crossing = []
    for d in range(1, nc):
        copy = pltpu.make_async_remote_copy(
            src_ref=out_ref.at[core],
            dst_ref=out_ref.at[core],
            send_sem=send_c.at[d],
            recv_sem=recv_c.at[d],
            device_id=(me, lax.rem(core + d, nc)),
            device_id_type=MESH,
        )
        copy.start()
        crossing.append(copy)
    for copy in scatter + spread:
        copy.wait_send()
    for copy in crossing:
        copy.wait()


def totals(parts, n, nc):
    rows = parts.shape[1]
    return pl.pallas_call(
        lambda *refs: total_kernel(n, nc, *refs),
        name="weight_totals",
        out_shape=jax.ShapeDtypeStruct((nc, n, rows, LANES), parts.dtype),
        in_specs=[pl.BlockSpec(memory_space=pltpu.VMEM)],
        out_specs=pl.BlockSpec(memory_space=pltpu.VMEM),
        scratch_shapes=[pltpu.VMEM((n, rows, LANES), parts.dtype)]
        + [pltpu.SemaphoreType.DMA((n,))] * 4
        + [pltpu.SemaphoreType.DMA((nc,))] * 2,
        compiler_params=pltpu.CompilerParams(collective_id=0, has_side_effects=True),
    )(parts)


def shards(tile_features, conv_weight, merge_weight, tissue, group_tiles, neighbours, merged_grad):
    chan_index = lax.axis_index("chan")
    local_groups = neighbours.shape[0]
    local_tiles = tile_features.shape[0]
    own_chan = tile_features.shape[1]
    own_merged = merged_grad.shape[1]
    extent = 2 * PIX
    local_ids = group_tiles % local_tiles
    own_picture = assemble(tile_features, local_ids, PIX)
    own_edges = boundary(own_picture)
    sides = []
    for direction in range(8):
        row_step = ROW_STEPS[direction]
        device_step = COLUMN_STEPS[direction] + 4 * row_step
        sending = own_edges[:, OPPOSITE[direction]]
        arrived = passed_along(sending, "tile", -device_step)
        blank = jnp.zeros((1, own_chan, extent), jnp.bfloat16)
        if row_step == 1:
            aligned = jnp.concatenate([arrived[1:], blank], axis=0)
        elif row_step == -1:
            aligned = jnp.concatenate([blank, arrived[:-1]], axis=0)
        else:
            aligned = arrived
        present_rows = (neighbours[:, direction] >= 0)[:, None, None]
        sides.append(jnp.where(present_rows, aligned, jnp.zeros((), jnp.bfloat16)))
    rim_flat = jnp.stack(sides, axis=2).reshape(local_groups, own_chan, 8 * extent)
    all_tiles, all_rims = (
        lax.all_gather(tile_features, "chan", axis=1, tiled=True),
        lax.all_gather(rim_flat, "chan", axis=1, tiled=True),
    )
    channels_all = all_tiles.shape[1]
    rim_cells = all_rims.reshape(local_groups, channels_all, 8, extent).transpose(0, 2, 1, 3)
    padded = framed(assemble(all_tiles, local_ids, PIX), rim_cells)
    conv_out = lax.conv_general_dilated(
        padded,
        conv_weight,
        (1, 1),
        "VALID",
        dimension_numbers=("NCHW", "OIHW", "NCHW"),
        preferred_element_type=jnp.float32,
    )
    tissue_rows = (
        jnp.take(tissue, local_ids.reshape(-1)).reshape(local_groups, 4).astype(jnp.float32)
    )
    hidden = (jnp.maximum(conv_out, 0.0) * tissue_map(tissue_rows, PIX)[:, None]).astype(
        jnp.bfloat16
    )
    hidden_blocks = to_blocks(hidden, PIX)
    merge_rows = lax.dynamic_slice_in_dim(merge_weight, chan_index * own_chan, own_chan, 0)
    every_block = lax.all_gather(hidden_blocks, "chan", axis=2, tiled=True)
    merge_columns = lax.dynamic_slice_in_dim(merge_weight, chan_index * own_merged, own_merged, 2)
    merged = jnp.einsum(
        "ckm,gkcq->gmq", merge_columns, every_block, preferred_element_type=jnp.float32
    ).astype(jnp.bfloat16)
    upstream = lax.all_gather(merged_grad, "chan", axis=1, tiled=True)
    grad_hidden = from_blocks(
        jnp.einsum("ckm,gmq->gkcq", merge_rows, upstream, preferred_element_type=jnp.float32), PIX
    )
    grad_pre = jnp.where(hidden > 0, grad_hidden, 0.0).astype(jnp.bfloat16)
    merge_term = jnp.einsum(
        "gmq,gkcq->ckm", upstream, hidden_blocks, preferred_element_type=jnp.float32
    )
    conv_term = lax.conv_general_dilated(
        padded,
        grad_pre,
        (1, 1),
        "VALID",
        dimension_numbers=("CNHW", "IOHW", "NCHW"),
        preferred_element_type=jnp.float32,
    )
    conv_term = conv_term.transpose(1, 0, 2, 3)
    n = lax.axis_size("tile")
    nc = lax.axis_size("chan")
    conv_rows = conv_term.transpose(2, 3, 0, 1).reshape(-1, LANES)
    merge_rows_part = merge_term.reshape(-1, LANES)
    stacked = jnp.concatenate([conv_rows, merge_rows_part], axis=0).astype(jnp.bfloat16)
    used = stacked.shape[0]
    rows = -(-used // (16 * n)) * 16
    parts = jnp.pad(stacked, ((0, rows * n - used), (0, 0))).reshape(n, rows, LANES)
    summed = totals(parts, n, nc).reshape(nc, n * rows, LANES)
    conv_count = conv_rows.shape[0]
    grad_conv = (
        summed[:, :conv_count]
        .reshape(nc, 3, 3, own_chan, channels_all)
        .transpose(0, 3, 4, 1, 2)
        .reshape(channels_all, channels_all, 3, 3)
        .astype(jnp.float32)
    )
    grad_merge = (
        summed[:, conv_count:used].reshape(merge_weight.shape).astype(jnp.float32)
    )
    return (merged, grad_conv, grad_merge)


def edge_picker():
    picks = np.zeros((PIX * PIX, 4 * PIX), np.float32)
    for i in range(PIX):
        picks[i, i] = 1
        picks[(PIX - 1) * PIX + i, PIX + i] = 1
        picks[i * PIX, 2 * PIX + i] = 1
        picks[i * PIX + PIX - 1, 3 * PIX + i] = 1
    return picks.astype(ml_dtypes.bfloat16)


def phase_picker():
    picks = np.zeros((2, 8, PIX, 2, 2, 4, PIX), np.float32)
    for side in range(2):
        for row in range(8):
            for x in range(PIX):
                picks[side, row, x, row % 2, x % 2, row // 2, 16 * side + x // 2] = 1
    return picks.reshape(512, 512).astype(ml_dtypes.bfloat16)


def column_picker():
    picks = np.zeros((2, 4 * PIX, 2, 16, PIX), np.float32)
    for r in range(2):
        for y in range(16):
            picks[0, 3 * PIX + 2 * y + r, r, y, 0] = 1
            picks[1, 2 * PIX + 2 * y + r, r, y, PIX - 1] = 1
    return picks.reshape(256, 1024).astype(ml_dtypes.bfloat16)


def row_picker():
    picks = np.zeros((2, 4, 4 * PIX, 4, 128), np.float32)
    for core in range(2):
        base = PIX * core
        for t in range(4):
            for x in range(PIX):
                at = 2 * x + t
                out = x if core == 1 else 96 + x
                if at == 0:
                    slot, lane = 2, base + PIX - 1
                elif at == 65:
                    slot, lane = 3, base
                else:
                    slot, lane = (at - 1) // PIX, base + (at - 1) % PIX
                picks[core, slot, lane, t, out] = 1
    return picks.reshape(2, 512, 512).astype(ml_dtypes.bfloat16)


def exchange_kernel(
    n, ids, stored, grad, weight, picks, full, grad_full, weight_full, side, cap,
    tiles, sides, caps, corners, send_own, recv_own, send_side, recv_side, send_cap, recv_cap,
):
    p = lax.axis_index("tile")
    k = lax.axis_index("chan")
    other = 1 - k
    toward = 1 - 2 * k
    barrier = pltpu.get_barrier_semaphore()

    def at(step):
        return lax.rem(p + step + n, n)

    def greet(row, core):
        pl.semaphore_signal(barrier, inc=1, device_id=(row, core), device_id_type=MESH)

    greet(p, other)
    for core in range(2):
        for step in (-1, 1):
            greet(at(step), core)
        for step in (3, 4, 5):
            greet(at(toward * step), core)
    count = stored.shape[0]
    for g in range(2):
        for column in range(2):
            for row in range(2):
                tiles[g, 2 * column + row] = stored[lax.rem(ids[g, 2 * row + column], count)]
    edge = dot(tiles[...].reshape(512, 1024), picks[...])
    lane = lax.broadcasted_iota(jnp.int32, (64, 128), 1)

    def edge_of(g, column, row):
        start = 64 * (4 * g + 2 * column + row)
        return edge[start : start + 64]

    bf = jnp.bfloat16
    for g in range(2):
        sides[g, 0] = jnp.where(
            lane < 96, edge_of(g, 0, 0), pltpu.roll(edge_of(g, 0, 1), 32, 1)
        ).astype(bf)
        sides[g, 1] = jnp.where(
            lane >= 96, edge_of(g, 1, 0), pltpu.roll(edge_of(g, 1, 1), 96, 1)
        ).astype(bf)
    for target in range(2):
        g = 1 - target
        caps[target] = jnp.where(
            lane < 32 + 32 * target,
            edge_of(g, 0, target),
            pltpu.roll(edge_of(g, 1, target), 32, 1),
        ).astype(bf)
        for column in range(2):
            corners[target, column] = edge_of(g, column, target).astype(bf)
    pl.semaphore_wait(barrier, 11)

    def send(src, dst, send_sem, recv_sem, row, core):
        copy = pltpu.make_async_remote_copy(
            src_ref=src,
            dst_ref=dst,
            send_sem=send_sem,
            recv_sem=recv_sem,
            device_id=(row, core),
            device_id_type=MESH,
        )
        copy.start()
        return copy

    half = pl.ds(pl.multiple_of(64 * k, 64), 64)
    wide = pl.ds(pl.multiple_of(128 * k, 128), 128)
    copies = []
    for g in range(2):
        for s, step in ((0, 1), (1, -1)):
            copies.append(
                send(
                    sides.at[g, 1 - s], side.at[s, half],
                    send_side.at[g, s], recv_side.at[s, k], at(step), g,
                )
            )
    for target, sign in ((1, 1), (0, -1)):
        copies.append(
            send(
                caps.at[target], cap.at[0, half],
                send_cap.at[target, 0], recv_cap.at[0, k], at(4 * sign), target,
            )
        )
        for slot, step, column in ((1, 5 if sign > 0 else -3, 1), (2, 3 if sign > 0 else -5, 0)):
            copies.append(
                send(
                    corners.at[target, column], cap.at[slot, half],
                    send_cap.at[target, slot], recv_cap.at[slot, k], at(step), target,
                )
            )
    copies.append(send(tiles.at[other], full.at[:, half], send_own.at[0], recv_own.at[0], p, other))
    copies.append(send(grad.at[other], grad_full.at[wide], send_own.at[1], recv_own.at[1], p, other))
    copies.append(send(weight, weight_full.at[k], send_own.at[2], recv_own.at[2], p, other))
    full[:, half] = tiles[k]
    grad_full[wide] = grad[k]
    weight_full[k] = weight[...]
    for copy in copies:
        copy.wait_send()
    copies[-1].wait_recv()
    copies[-2].wait_recv()
    copies[-3].wait_recv()

    def arrived(dst, recv_sem):
        pltpu.make_async_remote_copy(
            src_ref=dst,
            dst_ref=dst,
            send_sem=send_own.at[0],
            recv_sem=recv_sem,
            device_id=(p, other),
            device_id_type=MESH,
        ).wait_recv()

    for core in range(2):
        part = pl.ds(64 * core, 64)
        for s in range(2):
            arrived(side.at[s, part], recv_side.at[s, core])
        for slot in range(3):
            arrived(cap.at[slot, part], recv_cap.at[slot, core])


def exchange(ids, tiles, grad, weight, picks, n):
    bf = jnp.bfloat16
    vmem = pl.BlockSpec(memory_space=pltpu.VMEM)
    return pl.pallas_call(
        lambda *refs: exchange_kernel(n, *refs),
        name="exchange",
        out_shape=(
            jax.ShapeDtypeStruct((4, 128, 1024), bf),
            jax.ShapeDtypeStruct((256, 1024), bf),
            jax.ShapeDtypeStruct((2, 9, 64, 128), bf),
            jax.ShapeDtypeStruct((2, 128, 128), bf),
            jax.ShapeDtypeStruct((3, 128, 128), bf),
        ),
        in_specs=[pl.BlockSpec(memory_space=pltpu.SMEM)] + [vmem] * 4,
        out_specs=(vmem,) * 5,
        scratch_shapes=[
            pltpu.VMEM((2, 4, 64, 1024), bf),
            pltpu.VMEM((2, 2, 64, 128), bf),
            pltpu.VMEM((2, 64, 128), bf),
            pltpu.VMEM((2, 2, 64, 128), bf),
            pltpu.SemaphoreType.DMA((3,)),
            pltpu.SemaphoreType.DMA((3,)),
            pltpu.SemaphoreType.DMA((2, 2)),
            pltpu.SemaphoreType.DMA((2, 2)),
            pltpu.SemaphoreType.DMA((2, 3)),
            pltpu.SemaphoreType.DMA((3, 2)),
        ],
        compiler_params=pltpu.CompilerParams(
            collective_id=1, has_side_effects=True, vmem_limit_bytes=32 << 20
        ),
    )(ids, tiles, grad, weight, picks)


def dot(a, b):
    return jnp.dot(a, b, preferred_element_type=jnp.float32)


def dot_lanes(a, b):
    return lax.dot_general(a, b, (((1,), (1,)), ((), ())), preferred_element_type=jnp.float32)


def group_kernel(
    near_groups, ids, tissue, full, grad, weight, side, cap, mix, mix_turned, phases, columns, rows,
    merged, parts,
    phase, lr, taps, wide_weight, hidden, dpre, conv_sum,
):
    bf = jnp.bfloat16
    core = lax.axis_index("chan")
    count = tissue.shape[0]
    entry_of = (2, 3, core * -1 + 1, core * -2 + 6, core * -2 + 7)
    known = [near_groups[core, entry] for entry in entry_of]
    kinds = [tissue[lax.rem(ids[core, t], count)].astype(jnp.float32) for t in range(4)]
    spot = lax.broadcasted_iota(jnp.int32, (1, 1024), 1)
    east = (spot % 32) >= 16
    flags = jnp.where(
        spot >= 512, jnp.where(east, kinds[3], kinds[2]), jnp.where(east, kinds[1], kinds[0])
    )
    for ty in range(2):
        for j in range(4):
            lanes = pl.ds(256 * j, 256)
            picked = dot(full[ty, :, lanes], phases[:256]) + dot(full[2 + ty, :, lanes], phases[256:])
            out = pl.ds((4 * ty + j) * 128, 128)
            for q in range(4):
                phase[q, :, out] = picked[:, 128 * q : 128 * q + 128]
    zero = jnp.zeros((), bf)
    blank_side = jnp.zeros((), jnp.float32)
    near_left = jnp.where(known[0] >= 0, side[0].astype(jnp.float32), blank_side)
    near_right = jnp.where(known[1] >= 0, side[1].astype(jnp.float32), blank_side)
    near_cap = jnp.where(known[2] >= 0, cap[0].astype(jnp.float32), blank_side)
    left = [near_left.astype(bf), pltpu.roll(near_left, 32, 1).astype(bf)]
    right = [near_right.astype(bf), pltpu.roll(near_right, 96, 1).astype(bf)]
    for ty in range(2):
        picked = dot(left[ty], columns[:128]) + dot(right[ty], columns[128:])
        for r in range(2):
            lr[r, :, pl.ds(512 * ty, 512)] = picked[:, 512 * r : 512 * r + 512]
    rim = jnp.zeros((128, 512), jnp.float32)
    row_sources = (
        near_cap.astype(bf),
        pltpu.roll(near_cap, 96, 1).astype(bf),
        jnp.where(known[3] >= 0, cap[1], zero),
        jnp.where(known[4] >= 0, cap[2], zero),
    )
    for slot, source in enumerate(row_sources):
        rim += dot(source, rows[core, pl.ds(128 * slot, 128), :])
    lane = lax.broadcasted_iota(jnp.int32, (128, 1024), 1)
    first = (lane % 32) == 0
    final = (lane % 32) == 31
    narrow = lax.broadcasted_iota(jnp.int32, (128, 128), 1)
    for tx in range(4):
        for r in range(2):
            if tx == 0:
                base = jnp.where(first, lr[r], pltpu.roll(phase[2 * r + 1], 1, 1))
            elif tx == 1:
                base = phase[2 * r]
            elif tx == 2:
                base = phase[2 * r + 1]
            else:
                base = jnp.where(final, lr[r], pltpu.roll(phase[2 * r], 1023, 1))
            taps[pl.ds(((1 + r) * 4 + tx) * 128, 128), :] = base.astype(bf)
            corner = rim[:, 128 * tx : 128 * tx + 128]
            if r == 1:
                moved = pltpu.roll(base, 32, 1)
                at = pl.ds(tx * 128, 128)
                taps[at, 128:] = moved[:, 128:].astype(bf)
                taps[at, :128] = jnp.where(narrow < 32, corner, moved[:, :128]).astype(bf)
            else:
                moved = pltpu.roll(base, 992, 1)
                at = pl.ds((12 + tx) * 128, 128)
                taps[at, :896] = moved[:, :896].astype(bf)
                taps[at, 896:] = jnp.where(narrow >= 96, corner, moved[:, 896:]).astype(bf)
    for b in range(2):
        for i in range(3):
            blank = pl.ds((4 * i + (3 if b == 0 else 0)) * 128, 128)
            wide_weight[pl.ds(128 * b, 128), blank] = jnp.zeros((128, 128), bf)
            for j in range(3):
                for core in range(2):
                    wide_weight[pl.ds(128 * b + 64 * core, 64), pl.ds((4 * i + j + b) * 128, 128)] = (
                        weight[core, 3 * i + j]
                    )
    for a in range(2):
        at = pl.ds(256 * a, 256)
        pre = dot(wide_weight[...], taps[pl.ds(512 * a, 1536), :])
        kept = (jnp.maximum(pre, 0.0) * flags).astype(bf)
        hidden[at, :] = kept
        upstream = dot(mix[at, :], grad[...])
        dpre[at, :] = jnp.where(kept.astype(jnp.float32) > 0, upstream, 0.0).astype(bf)
    for h in range(2):
        merged[h] = dot(mix_turned[pl.ds(128 * h, 128), :], hidden[...]).astype(bf)
    for i in range(3):
        strip = jnp.zeros((256, 512), jnp.float32)
        for a in range(2):
            strip += dot_lanes(dpre[pl.ds(256 * a, 256), :], taps[pl.ds(512 * (a + i), 512), :])
        for j in range(3):
            conv_sum[pl.ds((3 * i + j) * 128, 128), :] = (
                strip[:128, 128 * j : 128 * j + 128] + strip[128:, 128 * j + 128 : 128 * j + 256]
            )
    for piece in range(32):
        parts[piece, 0:36] = conv_sum[pl.ds(36 * piece, 36), :]
        parts[piece, 36:48] = jnp.zeros((12, 128), jnp.float32)
    mixed = dot_lanes(hidden[...], grad[...])
    for piece in range(32):
        parts[piece, 48:64] = mixed[16 * piece : 16 * piece + 16, :128]
        parts[piece, 64:80] = mixed[16 * piece : 16 * piece + 16, 128:]


def group_step(near_groups, ids, tissue, *arrays):
    bf, f32 = jnp.bfloat16, jnp.float32
    vmem = pl.BlockSpec(memory_space=pltpu.VMEM)
    return pl.pallas_call(
        group_kernel,
        name="group_step",
        out_shape=(
            jax.ShapeDtypeStruct((2, 128, 1024), bf),
            jax.ShapeDtypeStruct((32, 80, 128), f32),
        ),
        in_specs=[pl.BlockSpec(memory_space=pltpu.SMEM)] * 3 + [vmem] * len(arrays),
        out_specs=(vmem, vmem),
        scratch_shapes=[
            pltpu.VMEM((4, 128, 1024), f32),
            pltpu.VMEM((2, 128, 1024), f32),
            pltpu.VMEM((2048, 1024), bf),
            pltpu.VMEM((256, 1536), bf),
            pltpu.VMEM((512, 1024), bf),
            pltpu.VMEM((512, 1024), bf),
            pltpu.VMEM((1152, 128), f32),
        ],
        compiler_params=pltpu.CompilerParams(vmem_limit_bytes=48 << 20),
    )(near_groups, ids, tissue, *arrays)


def finish_kernel(
    part_ref, mine_ref, conv_ref, mix_ref, merged_ref, out_ref, near, held, flat, mid, middle,
    tall, send_a, recv_a, send_b, recv_b, send_c, recv_c, send_d, recv_d, send_e, recv_e,
    chip_send, chip_recv,
):
    me = lax.axis_index("tile")
    core = lax.axis_index("chan")
    z = me // 4
    q = lax.rem(me, 4)
    other = 1 - core
    barrier = pltpu.get_barrier_semaphore()

    def beside(d):
        return lax.rem(q + d, 4)

    def above(d):
        return lax.rem(z + d, 4)

    def remote(src, dst, send_sem, recv_sem, row, column):
        copy = pltpu.make_async_remote_copy(
            src_ref=src,
            dst_ref=dst,
            send_sem=send_sem,
            recv_sem=recv_sem,
            device_id=(row, column),
            device_id_type=MESH,
        )
        copy.start()
        return copy

    pl.semaphore_signal(barrier, inc=1, device_id=(me, other), device_id_type=MESH)
    for d in range(1, 4):
        for row in (4 * z + beside(d), 4 * above(d) + q):
            pl.semaphore_signal(barrier, inc=1, device_id=(row, core), device_id_type=MESH)
    held[...] = part_ref[other].astype(held.dtype)
    pl.semaphore_wait(barrier, 7)

    over = remote(held, near, chip_send.at[0], chip_recv.at[0], me, other)
    swap = remote(
        mine_ref.at[other], merged_ref.at[core], chip_send.at[1], chip_recv.at[1], me, other
    )
    merged_ref[core] = mine_ref[core]
    over.wait()
    held[...] = (part_ref[core] + near[...].astype(jnp.float32)).astype(held.dtype)

    sent = []
    across = []
    for d in range(1, 4):
        across.append(
            remote(
                held.at[:, beside(d)], flat.at[d], send_a.at[d], recv_a.at[d],
                4 * z + beside(d), core,
            )
        )
    total = part_ref[core, :, q] + near[:, q].astype(jnp.float32)
    for d in range(1, 4):
        across[d - 1].wait_recv()
        total += flat[d].astype(jnp.float32)
    middle[...] = total
    mid[...] = total.astype(mid.dtype)
    along = []
    for d in range(1, 4):
        along.append(
            remote(
                mid.at[above(d)], tall.at[d], send_b.at[d], recv_b.at[d], 4 * above(d) + q, core
            )
        )
    last = middle[z]
    for d in range(1, 4):
        along[d - 1].wait_recv()
        last += tall[d].astype(jnp.float32)
    out_ref[core, z, q] = last.astype(out_ref.dtype)

    own = out_ref.at[core, z, q]
    column = out_ref.at[core, :, q]
    raised = []
    for d in range(1, 4):
        raised.append(remote(own, own, send_c.at[d], recv_c.at[d], 4 * above(d) + q, core))
    for copy in raised:
        copy.wait_recv()
    spread = []
    for d in range(1, 4):
        spread.append(
            remote(column, column, send_d.at[d], recv_d.at[d], 4 * z + beside(d), core)
        )
    crossing = [remote(column, column, send_e.at[0], recv_e.at[0], me, other)]
    for d in range(1, 4):
        spread[d - 1].wait_recv()
        column = out_ref.at[core, :, lax.rem(q + 4 - d, 4)]
        crossing.append(remote(column, column, send_e.at[d], recv_e.at[d], me, other))
    for copy in across + along + raised + spread:
        copy.wait_send()
    swap.wait()
    for copy in crossing:
        copy.wait()
    for piece in range(32):
        block = out_ref[piece // 16, (piece % 16) // 4, piece % 4].astype(jnp.float32)
        conv_ref[pl.ds(36 * piece, 36), :] = block[:36]
        mix_ref[pl.ds(16 * piece, 16), :128] = block[48:64]
        mix_ref[pl.ds(16 * piece, 16), 128:] = block[64:]


def finish(parts, mine):
    bf = jnp.bfloat16
    rows = parts.shape[3]
    vmem = pl.BlockSpec(memory_space=pltpu.VMEM)
    return pl.pallas_call(
        finish_kernel,
        name="finish",
        out_shape=(
            jax.ShapeDtypeStruct((1152, LANES), jnp.float32),
            jax.ShapeDtypeStruct((512, 2 * LANES), jnp.float32),
            jax.ShapeDtypeStruct(mine.shape, bf),
        ),
        in_specs=[vmem] * 2,
        out_specs=(vmem, vmem, vmem),
        scratch_shapes=[pltpu.VMEM((2, 4, 4, rows, LANES), bf)]
        + [pltpu.VMEM((4, 4, rows, LANES), bf)] * 3
        + [
            pltpu.VMEM((4, rows, LANES), bf),
            pltpu.VMEM((4, rows, LANES), jnp.float32),
            pltpu.VMEM((4, rows, LANES), bf),
        ]
        + [pltpu.SemaphoreType.DMA((4,))] * 10
        + [pltpu.SemaphoreType.DMA((2,))] * 2,
        compiler_params=pltpu.CompilerParams(
            collective_id=2, has_side_effects=True, vmem_limit_bytes=32 << 20
        ),
    )(parts, mine)


def group_per_core(
    tile_features, conv_weight, merge_weight, tissue, group_tiles, neighbours, merged_grad
):
    n = lax.axis_size("tile")
    full, grad_full, weight_full, side, cap = exchange(
        group_tiles,
        tile_features,
        merged_grad,
        conv_weight.transpose(2, 3, 0, 1).reshape(9, 64, 128),
        jnp.asarray(edge_picker()),
        n,
    )
    mix = merge_weight.transpose(1, 0, 2).reshape(512, 256)
    merged_all, parts = group_step(
        neighbours, group_tiles, tissue, full, grad_full, weight_full, side, cap, mix, mix.T,
        jnp.asarray(phase_picker()), jnp.asarray(column_picker()), jnp.asarray(row_picker()),
    )
    summed_conv, summed_mix, merged = finish(parts.reshape(2, 4, 4, 80, LANES), merged_all)
    grad_conv = summed_conv.reshape(3, 3, 128, 128).transpose(2, 3, 0, 1)
    grad_merge = summed_mix.reshape(4, 128, 256).transpose(1, 0, 2)
    return merged, grad_conv, grad_merge


def solution(mesh):
    placed = (
        P("tile", "chan", None),
        P("chan", None, None, None),
        P(),
        P("tile"),
        P("tile", None),
        P("tile", None),
        P("tile", "chan", None),
    )
    pairs = mesh.shape["chan"] == 2 and mesh.shape["tile"] == 16
    return jax.shard_map(
        group_per_core if pairs else shards,
        mesh=mesh,
        in_specs=placed,
        out_specs=(P("tile", "chan", None), P(), P()),
        check_vma=False,
    )
```
